32 devices in a mesh: groups: 2 (over y), tiles: 16 (over z, x, core).
Axes of the slice: x: 2, y: 2, z: 4, core: 2. Of those that a mesh axis runs over, the one named last changes fastest.
Arguments:
- raw: bfloat16 [16, 256, 2048], P(None, ('groups', 'tiles')), parts along dimension 1, may hold values from -40 to 40, as said below
- fir: float32 [64], replicated, may hold values from -0.75 to 0.75
- keep: int32 [16, 256], P(None, ('groups', 'tiles')), parts along dimension 1, may hold values 0 or 1
- table: int32 [16, 2], replicated, may hold values from 0 to 0, as said below
Outputs:
- stacks: bfloat16 [32, 128, 128, 256], P(('groups', 'tiles')), parts along dimension 0
The draws below stay inside these ranges and needn't reach their ends.
There are 2 independent parts, one for each index of `groups`. The reference program is written for one: setup_inputs(seed, part) draws one part's arguments, and reference() takes and returns one part's arrays. A program takes and returns all parts, laid end to end along the dimension named above; an argument that names none is the same for every part. Nothing has to cross between parts.
Inputs may be any that keep to these rules, and one draw needn't show every extreme that they name: `table`: each row holds r <= c. `raw`: a common motion of all channels plus independent noise.
All inputs are finite; a program needn't handle non-finite values. No bound on the sum of `keep` on one device may be relied on, other than what follows from the above.
Results may differ from the reference program's by a relative error of at most 0.0053.
Values may be sent and summed in bfloat16 or wider, within the bound.
A program may use at most 128 MiB of HBM per device.

```python
import jax
import jax.numpy as jnp
from jax import lax

WINDOWS = 16
TILE = 128
SEG = 512
LAGS = 256
TAPS = 64
DEC = 4
RAW = 2048
NBIN = 256
CHANNELS = 128
BLOCKS = 1
N_TILES = 16


def draw_raw(key, part):
    noise_key = jax.random.fold_in(key, 11)
    common_key = jax.random.fold_in(key, 12)
    gain_key = jax.random.fold_in(key, 13)
    noise = jax.random.normal(noise_key, (WINDOWS, CHANNELS, RAW), jnp.float32)
    common = jax.random.normal(common_key, (WINDOWS, 1, RAW), jnp.float32)
    gain = jnp.exp(jax.random.uniform(gain_key, (1, CHANNELS, 1), jnp.float32, -0.7, 0.7))
    return jnp.clip(noise + 2.0 * gain * common, -40.0, 40.0).astype(jnp.bfloat16)


def draw_table(key, part):
    pair = jax.random.randint(jax.random.fold_in(key, 21), (N_TILES, 2), 0, BLOCKS)
    low = jnp.minimum(pair[:, 0], pair[:, 1])
    high = jnp.maximum(pair[:, 0], pair[:, 1])
    high = high.at[0].set(BLOCKS - 1)
    return jnp.stack([low, high], 1).astype(jnp.int32)


def touch_ends(drawn, own_key, low, largest):
    place = [jax.random.randint(jax.random.fold_in(own_key, axis), (), 0, length) for axis, length in enumerate(drawn.shape)]
    widest = drawn.shape.index(max(drawn.shape))
    neighbour = place[:widest] + [(place[widest] + 1) % drawn.shape[widest]] + place[widest + 1:]
    return drawn.at[tuple(place)].set(low).at[tuple(neighbour)].set(largest)


def gaussian(own_key, shape, spread, reach, kind=jnp.bfloat16):
    return jnp.clip(spread * jax.random.normal(own_key, shape, jnp.float32), -reach, reach).astype(kind)


def setup_inputs(seed: int = 0, part: int = 0) -> dict:
    keys = jax.random.split(jax.random.key(seed), 5)
    part_splits = jax.random.split(jax.random.fold_in(keys[4], part), 5)
    raw = draw_raw(jax.random.fold_in(jax.random.fold_in(keys[4], part), 71), part)
    fir = gaussian(keys[1], (TAPS,), TAPS ** -0.5, 0.75, jnp.float32)
    keep = touch_ends((jax.random.randint(part_splits[2], (WINDOWS, CHANNELS), 0, 8) < 7).astype(jnp.int32), jax.random.fold_in(part_splits[2], 1), 0, 1)
    table = draw_table(jax.random.fold_in(keys[4], 71), part)
    return dict(raw=raw, fir=fir, keep=keep, table=table)


def filter_band(fir):
    period = 2 * RAW + TAPS
    pattern = jnp.concatenate([fir[:1], jnp.zeros((period - TAPS,), jnp.float32), fir[1:][::-1]])
    tiled = jnp.tile(pattern, SEG)[:SEG * (period - DEC)].reshape(SEG, period - DEC)
    return tiled[:, :RAW]

def filter_block(raw, fir):
    band = filter_band(fir)
    return jnp.einsum('wcm,nm->wcn', raw.astype(jnp.float32), band, precision=lax.Precision.HIGHEST)

def dft_tables():
    steps = jnp.arange(SEG, dtype=jnp.int32)
    freqs = jnp.arange(NBIN, dtype=jnp.int32)
    angle = 2.0 * jnp.pi / SEG * jnp.mod(steps[:, None] * freqs[None, :], SEG).astype(jnp.float32)
    return (jnp.cos(angle), jnp.sin(angle))

def whiten(decimated, keep):
    cosine, sine = dft_tables()
    real_part = jnp.einsum('wcn,nf->wcf', decimated, cosine, precision=lax.Precision.HIGHEST)
    imag_part = -jnp.einsum('wcn,nf->wcf', decimated, sine, precision=lax.Precision.HIGHEST)
    power = real_part * real_part + imag_part * imag_part
    level = lax.optimization_barrier(jnp.mean(power, -1, keepdims=True))
    scale = keep.astype(jnp.float32)[..., None] / jnp.sqrt(0.5 * power + 0.5 * level + 1e-05)
    return jnp.concatenate([real_part * scale, imag_part * scale], -1).astype(jnp.bfloat16)

def cross_tile(rows, cols):
    half = rows.shape[-1] // 2
    row_re, row_im = (rows[..., :half], rows[..., half:])
    col_re, col_im = (cols[..., :half], cols[..., half:])
    cross_re = jnp.einsum('wif,wjf->ijf', row_re, col_re, preferred_element_type=jnp.float32)
    cross_re = cross_re + jnp.einsum('wif,wjf->ijf', row_im, col_im, preferred_element_type=jnp.float32)
    cross_im = jnp.einsum('wif,wjf->ijf', row_re, col_im, preferred_element_type=jnp.float32)
    cross_im = cross_im - jnp.einsum('wif,wjf->ijf', row_im, col_re, preferred_element_type=jnp.float32)
    return jnp.concatenate([cross_re, cross_im], -1).astype(jnp.bfloat16)

def lag_table():
    freqs = jnp.arange(NBIN, dtype=jnp.int32)
    shifts = jnp.arange(LAGS, dtype=jnp.int32) - LAGS // 2
    angle = 2.0 * jnp.pi / SEG * jnp.mod(freqs[:, None] * shifts[None, :], SEG).astype(jnp.float32)
    weight = jnp.where(freqs == 0, 1.0, 2.0).astype(jnp.float32)[:, None] / jnp.sqrt(jnp.float32(WINDOWS * NBIN))
    return jnp.concatenate([weight * jnp.cos(angle), -weight * jnp.sin(angle)], 0).astype(jnp.bfloat16)

def reference(raw, fir, keep, table):
    filtered = filter_block(raw, fir)
    common = lax.optimization_barrier(jnp.mean(filtered, 1, keepdims=True))
    whitened = whiten(filtered - common, keep)
    lags = lag_table()

    def one_tile(entry):
        rows = lax.dynamic_slice_in_dim(whitened, (entry[0] * TILE).astype(jnp.int32), TILE, 1)
        cols = lax.dynamic_slice_in_dim(whitened, (entry[1] * TILE).astype(jnp.int32), TILE, 1)
        cross = cross_tile(rows, cols).reshape(TILE * TILE, 2 * NBIN)
        return jnp.dot(cross, lags, preferred_element_type=jnp.float32).astype(jnp.bfloat16).reshape(TILE, TILE, LAGS)
    return lax.map(one_tile, table)
```

```python
import functools

import jax
import jax.numpy as jnp
import numpy as np
from jax import lax
from jax.experimental import pallas as pl
from jax.experimental.pallas import tpu as pltpu
from jax.sharding import PartitionSpec as P

WINDOWS = 16
TILE = 128
SEG = 512
LAGS = 256
TAPS = 64
DEC = 4
RAW = 2048
NBIN = 256
SPAN = 640
STRIDE = 521
PIECES = 4


def split2(x):
    high = x.astype(jnp.bfloat16)
    return high, (x - high.astype(jnp.float32)).astype(jnp.bfloat16)


def split3(x):
    high = x.astype(jnp.bfloat16)
    rest = x - high.astype(jnp.float32)
    middle = rest.astype(jnp.bfloat16)
    return high, middle, (rest - middle.astype(jnp.float32)).astype(jnp.bfloat16)


def contract(a, b, left, right):
    return lax.dot_general(a, b, (((left,), (right,)), ((), ())), preferred_element_type=jnp.float32)


def dft_tables():
    angle = 2.0 * np.pi / SEG * np.mod(np.arange(SEG)[:, None] * np.arange(NBIN)[None, :], SEG)
    table = np.concatenate([np.cos(angle), -np.sin(angle)], 1).astype(np.float32)
    high = table.astype(jnp.bfloat16)
    low = (table - high.astype(np.float32)).astype(jnp.bfloat16)
    return jnp.asarray(np.concatenate([high, low], 0))


def lag_table():
    freqs = np.arange(NBIN)
    shifts = np.arange(LAGS) - LAGS // 2
    angle = 2.0 * np.pi / SEG * np.mod(freqs[:, None] * shifts[None, :], SEG)
    weight = np.where(freqs == 0, 1.0, 2.0)[:, None] / np.sqrt(WINDOWS * NBIN)
    table = np.concatenate([weight * np.cos(angle), -weight * np.sin(angle)], 0)
    return jnp.asarray(table.astype(np.float32).astype(jnp.bfloat16))


def filter_rows(raw_ref, taps_ref):
    rows = raw_ref.shape[0] * raw_ref.shape[1]
    raw = raw_ref[...].astype(jnp.float32).reshape(rows, RAW).astype(jnp.bfloat16)
    taps = jnp.broadcast_to(taps_ref[...], (8, TAPS))
    places = lax.broadcasted_iota(jnp.int32, (TAPS, SPAN), 0) + lax.broadcasted_iota(jnp.int32, (TAPS, SPAN), 1)
    pick = jnp.where(places == TILE, 1.0, 0.0).astype(jnp.bfloat16)
    spread = sum(contract(part, pick, 1, 0) for part in split3(taps)[::-1])
    band = jnp.broadcast_to(spread[:1], (TILE, SPAN))
    index = lax.broadcasted_iota(jnp.int32, (TILE, SPAN), 0)
    for bit in range(7):
        band = jnp.where((index >> bit) & 1 == 1, pltpu.roll(band, DEC << bit, 1), band)
    pieces = [jnp.concatenate([jnp.zeros((rows, TILE), jnp.bfloat16), raw[:, :SEG]], 1)]
    for block in range(1, RAW // SEG):
        pieces.append(raw[:, block * SEG - TILE : (block + 1) * SEG])
    spans = jnp.concatenate(pieces, 0)
    out = sum(contract(spans, part, 1, 1) for part in split3(band)[::-1])
    return jnp.concatenate([out[b * rows : (b + 1) * rows] for b in range(RAW // SEG)], 1)


def whiten_rows(decimated, keep, table_ref):
    high, low = split2(decimated)
    table_high = table_ref[:SEG, :]
    spectrum = contract(low, table_high, 1, 0) + contract(high, table_ref[SEG:, :], 1, 0)
    spectrum = spectrum + contract(high, table_high, 1, 0)
    real_part, imag_part = spectrum[:, :NBIN], spectrum[:, NBIN:]
    power = real_part * real_part + imag_part * imag_part
    level = jnp.mean(power, -1, keepdims=True)
    scale = keep.astype(jnp.float32) * lax.rsqrt(0.5 * power + 0.5 * level + 1e-05)
    return jnp.concatenate([real_part * scale, imag_part * scale], 1).astype(jnp.bfloat16)


def arrange(piece_ref, spectra_ref):
    members, rows = piece_ref.shape[:2]
    width = rows // WINDOWS
    for pair in range(WINDOWS // 2):
        for quarter in range(4):
            block = piece_ref[:, pair * 2 * width : (pair + 1) * 2 * width, quarter * 128 : (quarter + 1) * 128]
            block = block.astype(jnp.float32)
            for half in range(2):
                turned = block[:, half * width : (half + 1) * width].reshape(members * width, 128).T
                start = (quarter % 2) * 128 * 32 + (quarter // 2) * WINDOWS + pair * 2 + half
                spectra_ref[pl.ds(start, 128, 32), :] = turned


def stack_kernel(same, per_step, *refs):
    if same:
        rows_ref, lag_ref, out_ref, cross_ref, row_spec = refs
    else:
        _, rows_ref, cols_ref, lag_ref, out_ref, cross_ref, row_spec, col_spec = refs

    @pl.when(pl.program_id(0) == 0)
    def _():
        arrange(rows_ref, row_spec)
        if not same:
            arrange(cols_ref, col_spec)

        def one_bin(f, carry):
            start = pl.multiple_of(f * 32, 32)
            left = row_spec[pl.ds(start, 32), :]
            right = left if same else col_spec[pl.ds(start, 32), :]
            turned = jnp.concatenate([right[WINDOWS:], -right[:WINDOWS]], 0)
            both = jnp.concatenate([right, turned], 1).astype(jnp.bfloat16)
            cross = contract(left.astype(jnp.bfloat16), both, 0, 0)
            cross_ref[pl.ds(f, TILE, STRIDE), :] = cross[:, :TILE]
            cross_ref[pl.ds(f + NBIN, TILE, STRIDE), :] = cross[:, TILE:]
            return carry

        lax.fori_loop(0, NBIN, one_bin, 0, unroll=64)

    base = pl.program_id(0) * per_step
    for group in range(per_step // 4):
        picked = []
        for member in range(4):
            start = (base + group * 4 + member) * STRIDE
            picked.append(cross_ref[pl.ds(start, 2 * NBIN), :].astype(jnp.bfloat16))
        stacked = contract(jnp.concatenate(picked, 1), lag_ref[...], 0, 0)
        out_ref[group * 4 : group * 4 + 4] = stacked.reshape(4, TILE, LAGS).astype(jnp.bfloat16)


def stack(gathered, table):
    members = TILE * WINDOWS // gathered.shape[1]
    same = gathered.shape[0] == members
    per_step = 32
    block = (members,) + gathered.shape[1:]
    spectra = pltpu.VMEM((2 * NBIN * WINDOWS, TILE), jnp.float32)
    if same:
        prefetch = []
        sides = [pl.BlockSpec(block, lambda s: (0, 0, 0))]
    else:
        prefetch = [table[lax.axis_index("tiles")]]
        sides = [
            pl.BlockSpec(block, lambda s, entry: (entry[0], 0, 0)),
            pl.BlockSpec(block, lambda s, entry: (entry[1], 0, 0)),
        ]
    return pl.pallas_call(
        functools.partial(stack_kernel, same, per_step),
        out_shape=jax.ShapeDtypeStruct((TILE, TILE, LAGS), jnp.bfloat16),
        grid_spec=pltpu.PrefetchScalarGridSpec(
            num_scalar_prefetch=len(prefetch),
            grid=(TILE // per_step,),
            in_specs=sides + [pl.BlockSpec((2 * NBIN, LAGS), lambda s, *entry: (0, 0))],
            out_specs=pl.BlockSpec((per_step, TILE, LAGS), lambda s, *entry: (s, 0, 0)),
            scratch_shapes=[pltpu.VMEM((TILE * STRIDE, TILE), jnp.float32)] + [spectra] * len(sides),
        ),
        compiler_params=pltpu.CompilerParams(vmem_limit_bytes=60 << 20),
        cost_estimate=pl.CostEstimate(flops=10 << 30, bytes_accessed=12 << 20, transcendentals=0),
    )(*prefetch, *[gathered] * len(sides), lag_table())


def other_core(me):
    return me + 1 - 2 * (me % 2)


def other_chip(me):
    return me + 2 - 4 * ((me // 2) % 2)


def remote(source, target, send, receive, peer):
    return pltpu.make_async_remote_copy(
        src_ref=source,
        dst_ref=target,
        send_sem=send,
        recv_sem=receive,
        device_id={"tiles": peer},
        device_id_type=pl.DeviceIdType.MESH,
    )


def front_kernel(
    devices, raw_hbm, taps_ref, keep_ref, table_hbm, out_ref,
    raw_ref, table_ref, load_sem, sum_buf, part_buf, common_buf, held,
    part_send, part_recv, common_send, common_recv,
    right_send, left_send, chip_send, core_send, held_recv, local_sem,
):
    me = lax.axis_index("tiles")
    channels = raw_ref.shape[1]
    rows = WINDOWS * channels
    barrier = pltpu.get_barrier_semaphore()
    all_owners = devices == WINDOWS

    def greet(k, carry):
        pl.semaphore_signal(
            barrier, inc=1, device_id={"tiles": (me + k) % devices}, device_id_type=pl.DeviceIdType.MESH
        )
        return carry

    lax.fori_loop(1, devices, greet, 0)
    load_raw = pltpu.make_async_copy(raw_hbm, raw_ref, load_sem.at[0])
    load_raw.start()
    load_table = pltpu.make_async_copy(table_hbm, table_ref, load_sem.at[1])
    load_table.start()
    load_raw.wait()
    filtered = filter_rows(raw_ref, taps_ref).reshape(WINDOWS, channels, SEG)
    sum_buf[...] = jnp.sum(filtered, 1, keepdims=True)
    pl.semaphore_wait(barrier, devices - 1)

    def part_copy(owner, slot):
        return remote(sum_buf.at[owner], part_buf.at[slot], part_send.at[owner], part_recv.at[slot], owner)

    def common_copy(owner, peer):
        return remote(common_buf.at[owner], common_buf.at[owner], common_send.at[peer], common_recv.at[owner], peer)

    def send_part(k, carry):
        owner = (me + k) % WINDOWS

        @pl.when(owner != me)
        def _():
            part_copy(owner, me).start()

        return carry

    lax.fori_loop(1 if all_owners else 0, WINDOWS, send_part, 0)

    @pl.when(me < WINDOWS)
    def _():
        part_buf[me] = sum_buf[me]

        def take(k, carry):
            part_copy(me, (me + k) % devices).wait_recv()
            return carry

        lax.fori_loop(1, devices, take, 0)
        common_buf[me] = jnp.sum(part_buf[...], 0)

        def give(k, carry):
            common_copy(me, (me + k) % devices).start()
            return carry

        lax.fori_loop(1, devices, give, 0)

    def take_common(k, carry):
        owner = (me + k) % WINDOWS

        @pl.when(owner != me)
        def _():
            common_copy(owner, me).wait_recv()

        return carry

    lax.fori_loop(1 if all_owners else 0, WINDOWS, take_common, 0)
    common = common_buf[...] / (channels * devices)
    decimated = (filtered - common).reshape(rows, SEG)
    keep = jnp.broadcast_to(keep_ref[...].astype(jnp.float32).T[:, :, None], (WINDOWS, channels, NBIN))
    load_table.wait()
    whitened = whiten_rows(decimated, keep.reshape(rows, NBIN), table_ref)
    held[me] = whitened.reshape(PIECES, rows // PIECES, 2 * NBIN)

    depth = devices // 4
    q, low = me // 4, me % 4
    chip, core = other_chip(me), other_core(me)

    def block_copy(block, piece, send, peer):
        return remote(held.at[block, piece], held.at[block, piece], send, held_recv.at[block, piece], peer)

    def to_right(level, piece):
        return block_copy(4 * level + low, piece, right_send.at[level, piece], (me + 4) % devices)

    def to_left(level, piece):
        return block_copy(4 * level + low, piece, left_send.at[level, piece], (me + devices - 4) % devices)

    def to_chip(level, piece):
        return block_copy(4 * level + low, piece, chip_send.at[level, piece], chip)

    def to_core(block, piece):
        return block_copy(block, piece, core_send.at[block // 2, piece], core)

    def local_copy(block, piece):
        part = rows // PIECES
        return pltpu.make_async_copy(
            held.at[block, piece], out_ref.at[block, pl.ds(piece * part, part)], local_sem.at[block, piece]
        )

    def arrived(block, piece):
        to_core(block, piece).wait_recv()
        local_copy(block, piece).start()

    def line_block(level, piece, forward, go):
        block = 4 * level + low
        arrived(block, piece)

        @pl.when(go)
        def _():
            forward(level, piece).start()

        to_chip(level, piece).start()
        to_core(block, piece).start()

    def chip_block(level, piece):
        block = 4 * level + other_chip(low)
        arrived(block, piece)
        to_core(block, piece).start()

    for piece in range(PIECES):
        @pl.when(q < depth - 1)
        def _():
            to_right(q, piece).start()

        @pl.when(q > 0)
        def _():
            to_left(q, piece).start()

        to_chip(q, piece).start()

    for piece in range(PIECES):
        to_core(me, piece).start()
        local_copy(me, piece).start()

    def step(d, carry):
        for piece in range(PIECES):
            @pl.when(q - d >= 0)
            def _():
                line_block(q - d, piece, to_right, q < depth - 1)

            @pl.when(q + d < depth)
            def _():
                line_block(q + d, piece, to_left, q > 0)

        for piece in range(PIECES):
            @pl.when(d == 1)
            def _():
                chip_block(q, piece)

            @pl.when((d > 1) & (q - d + 1 >= 0))
            def _():
                chip_block(q - d + 1, piece)

            @pl.when((d > 1) & (q + d - 1 < depth))
            def _():
                chip_block(q + d - 1, piece)

        return carry

    lax.fori_loop(1, depth + 1, step, 0)

    def from_core(pair, carry):
        for piece in range(PIECES):
            arrived(2 * pair + core % 2, piece)
        return carry

    lax.fori_loop(0, 2 * depth, from_core, 0)

    def finish(level, carry):
        for piece in range(PIECES):
            @pl.when((level <= q) & (q < depth - 1))
            def _():
                to_right(level, piece).wait_send()

            @pl.when((level >= q) & (q > 0))
            def _():
                to_left(level, piece).wait_send()

            to_chip(level, piece).wait_send()
            to_core(4 * level + low, piece).wait_send()
            to_core(4 * level + other_chip(low), piece).wait_send()
        return carry

    lax.fori_loop(0, depth, finish, 0)

    def drain_part(k, carry):
        owner = (me + k) % WINDOWS

        @pl.when(owner != me)
        def _():
            part_copy(owner, me).wait_send()

        return carry

    lax.fori_loop(1 if all_owners else 0, WINDOWS, drain_part, 0)

    @pl.when(me < WINDOWS)
    def _():
        def drain(k, carry):
            common_copy(me, (me + k) % devices).wait_send()
            return carry

        lax.fori_loop(1, devices, drain, 0)

    def settle(block, carry):
        for piece in range(PIECES):
            local_copy(block, piece).wait()
        return carry

    lax.fori_loop(0, devices, settle, 0)


def front(devices, raw, fir, keep):
    rows = raw.shape[0] * raw.shape[1]
    depth = devices // 4
    dma = pltpu.SemaphoreType.DMA
    vmem = pl.BlockSpec(memory_space=pltpu.VMEM)
    hbm = pl.BlockSpec(memory_space=pl.ANY)
    line = pltpu.VMEM((WINDOWS, 1, SEG), jnp.float32)
    return pl.pallas_call(
        functools.partial(front_kernel, devices),
        out_shape=jax.ShapeDtypeStruct((devices, rows, 2 * NBIN), jnp.bfloat16),
        in_specs=[hbm, vmem, vmem, hbm],
        out_specs=pl.BlockSpec(memory_space=pl.ANY),
        scratch_shapes=[
            pltpu.VMEM(raw.shape, jnp.bfloat16), pltpu.VMEM((2 * SEG, 2 * NBIN), jnp.bfloat16), dma((2,)),
            line, pltpu.VMEM((devices, 1, SEG), jnp.float32), line,
            pltpu.VMEM((devices, PIECES, rows // PIECES, 2 * NBIN), jnp.bfloat16),
            dma((WINDOWS,)), dma((devices,)), dma((devices,)), dma((WINDOWS,)),
            dma((depth, PIECES)), dma((depth, PIECES)), dma((depth, PIECES)), dma((2 * depth, PIECES)),
            dma((devices, PIECES)), dma((devices, PIECES)),
        ],
        compiler_params=pltpu.CompilerParams(
            collective_id=0, has_side_effects=True, vmem_limit_bytes=60 << 20
        ),
    )(raw, fir.reshape(1, TAPS), keep.T, dft_tables())


def piece_tables():
    angle = 2.0 * np.pi / SEG * np.mod(np.arange(SEG)[:, None] * np.arange(NBIN)[None, :], SEG)
    bins = NBIN // PIECES
    cosine, sine = np.cos(angle).reshape(SEG, PIECES, bins), -np.sin(angle).reshape(SEG, PIECES, bins)
    table = np.concatenate([cosine, sine], 2).reshape(SEG, 2 * NBIN).astype(np.float32)
    high = table.astype(jnp.bfloat16)
    low = (table - high.astype(np.float32)).astype(jnp.bfloat16)
    return jnp.asarray(np.concatenate([high, low], 0))


def whiten_pieces(decimated, keep, table_ref):
    high, low = split2(decimated)
    table_high = table_ref[:SEG, :]
    spectrum = contract(low, table_high, 1, 0) + contract(high, table_ref[SEG:, :], 1, 0)
    spectrum = spectrum + contract(high, table_high, 1, 0)
    width = 2 * NBIN // PIECES
    parts = [spectrum[:, p * width : (p + 1) * width] for p in range(PIECES)]
    squares = [part * part for part in parts]
    level = jnp.sum(sum(squares), -1, keepdims=True) / NBIN
    whitened = []
    for part, square in zip(parts, squares):
        power = square + pltpu.roll(square, width // 2, 1)
        scale = keep * lax.rsqrt(0.5 * power + 0.5 * level + 1e-05)
        whitened.append((part * scale).astype(jnp.bfloat16))
    return whitened


def tile_kernel(
    devices, raw_hbm, taps_hbm, keep_hbm, table_hbm, cross_ref,
    raw_ref, taps_ref, keep_ref, table_ref, load_sem, sum_buf, part_buf, common_buf, held, spectra_ref,
    part_send, part_recv, common_send, common_recv,
    line_send, chip_send, core_send, held_recv,
):
    me = lax.axis_index("tiles")
    channels = raw_ref.shape[1]
    rows = WINDOWS * channels
    barrier = pltpu.get_barrier_semaphore()

    def greet(k, carry):
        pl.semaphore_signal(
            barrier, inc=1, device_id={"tiles": (me + k) % devices}, device_id_type=pl.DeviceIdType.MESH
        )
        return carry

    lax.fori_loop(1, devices, greet, 0)
    load_raw = pltpu.make_async_copy(raw_hbm, raw_ref, load_sem.at[0])
    load_raw.start()
    load_taps = pltpu.make_async_copy(taps_hbm, taps_ref, load_sem.at[2])
    load_taps.start()
    load_keep = pltpu.make_async_copy(keep_hbm, keep_ref, load_sem.at[3])
    load_keep.start()
    load_table = pltpu.make_async_copy(table_hbm, table_ref, load_sem.at[1])
    load_table.start()
    load_taps.wait()
    load_raw.wait()
    filtered = filter_rows(raw_ref, taps_ref).reshape(WINDOWS, channels, SEG)
    sum_buf[...] = jnp.sum(filtered, 1, keepdims=True)
    pl.semaphore_wait(barrier, devices - 1)

    def part_copy(owner, slot):
        return remote(sum_buf.at[owner], part_buf.at[slot], part_send.at[owner], part_recv.at[slot], owner)

    def common_copy(owner, peer):
        return remote(common_buf.at[owner], common_buf.at[owner], common_send.at[peer], common_recv.at[owner], peer)

    def send_part(k, carry):
        part_copy((me + k) % devices, me).start()
        return carry

    lax.fori_loop(1, devices, send_part, 0)
    part_buf[me] = sum_buf[me]

    def take(k, carry):
        part_copy(me, (me + k) % devices).wait_recv()
        return carry

    lax.fori_loop(1, devices, take, 0)
    common_buf[me] = jnp.sum(part_buf[...], 0)

    def give(k, carry):
        common_copy(me, (me + k) % devices).start()
        return carry

    lax.fori_loop(1, devices, give, 0)

    def take_common(k, carry):
        common_copy((me + k) % devices, me).wait_recv()
        return carry

    lax.fori_loop(1, devices, take_common, 0)
    common = common_buf[...] / (channels * devices)
    decimated = (filtered - common).reshape(rows, SEG)
    load_keep.wait()
    keep = jnp.broadcast_to(keep_ref[...].astype(jnp.float32).T[:, :, None], (WINDOWS, channels, 128))
    load_table.wait()
    whitened = whiten_pieces(decimated, keep.reshape(rows, 128), table_ref)
    for piece in range(PIECES):
        held[me, piece] = whitened[piece]

    level, chip, core = me // 4, (me // 2) % 2, me % 2
    levels = [level, level + 1 - 2 * (level % 2), (level + 2) % 4, 3 - level]

    def at(line, chip_off, core_off):
        return 4 * levels[line] + 2 * (chip + chip_off - 2 * chip * chip_off) + core + core_off - 2 * core * core_off

    def block_copy(block, piece, send, peer):
        return remote(held.at[block, piece], held.at[block, piece], send, held_recv.at[block, piece], peer)

    def to_line(line, piece):
        return block_copy(me, piece, line_send.at[line, piece], at(line, 0, 0))

    def to_chip(line, piece):
        return block_copy(at(line, 0, 0), piece, chip_send.at[line, piece], at(0, 1, 0))

    def to_core(line, chip_off, piece):
        return block_copy(at(line, chip_off, 0), piece, core_send.at[line, chip_off, piece], at(0, 0, 1))

    def arrived(line, chip_off, core_off, piece):
        block = at(line, chip_off, core_off)
        block_copy(block, piece, held_recv.at[block, piece], me).wait_recv()

    def from_line(piece):
        for line in (1, 2, 3):
            arrived(line, 0, 0, piece)
            to_chip(line, piece).start()
            to_core(line, 0, piece).start()

    def from_chip(piece):
        for line in range(4):
            arrived(line, 1, 0, piece)
            to_core(line, 1, piece).start()

    def from_core(piece):
        for chip_off in range(2):
            for line in range(4):
                arrived(line, chip_off, 1, piece)

    bins = NBIN // PIECES

    def turn(piece):
        for pair in range(WINDOWS // 2):
            block = held[:, piece, pair * 2 * channels : (pair + 1) * 2 * channels, :].astype(jnp.float32)
            for half in range(2):
                turned = block[:, half * channels : (half + 1) * channels].reshape(devices * channels, 2 * bins).T
                window = pair * 2 + half
                spectra_ref[pl.ds(window, bins, 2 * WINDOWS), :] = turned[:bins]
                spectra_ref[pl.ds(WINDOWS + window, bins, 2 * WINDOWS), :] = turned[bins:]

    def multiply(piece, first, count):
        place = lax.broadcasted_iota(jnp.int32, (TILE, 8 * 2 * WINDOWS), 1) // (2 * WINDOWS)

        def eight_bins(g, carry):
            start = pl.multiple_of(g * 16 * WINDOWS, 16 * WINDOWS)
            right = spectra_ref[pl.ds(start, 16 * WINDOWS), :]
            split = right.reshape(8, 2, WINDOWS, TILE)
            turned = jnp.concatenate([split[:, 1:], -split[:, :1]], 1).reshape(16 * WINDOWS, TILE)
            both = jnp.concatenate([right, turned], 1).astype(jnp.bfloat16)
            left = right.T
            picked = [jnp.where(place == k, left, 0.0).astype(jnp.bfloat16) for k in range(8)]
            cross = contract(jnp.concatenate(picked, 0), both, 1, 0)
            for k in range(8):
                f = piece * bins + g * 8 + k
                cross_ref[pl.ds(f, TILE, STRIDE), :] = cross[k * TILE : (k + 1) * TILE, :TILE]
                cross_ref[pl.ds(f + NBIN, TILE, STRIDE), :] = cross[k * TILE : (k + 1) * TILE, TILE:]
            return carry

        lax.fori_loop(first // 8, (first + count) // 8, eight_bins, 0, unroll=count // 8)

    for piece in range(PIECES):
        for line in (1, 2, 3):
            to_line(line, piece).start()
        to_chip(0, piece).start()
        to_core(0, 0, piece).start()

    half = bins // 2
    from_line(0)
    from_chip(0)
    from_line(1)
    from_core(0)
    for piece in range(PIECES):
        turn(piece)
        multiply(piece, 0, half)
        if piece + 1 < PIECES:
            from_chip(piece + 1)
        if piece + 2 < PIECES:
            from_line(piece + 2)
        multiply(piece, half, half)
        if piece + 1 < PIECES:
            from_core(piece + 1)

    for piece in range(PIECES):
        for line in range(4):
            if line:
                to_line(line, piece).wait_send()
            to_chip(line, piece).wait_send()
            to_core(line, 0, piece).wait_send()
            to_core(line, 1, piece).wait_send()

    def drain(k, carry):
        part_copy((me + k) % devices, me).wait_send()
        common_copy(me, (me + k) % devices).wait_send()
        return carry

    lax.fori_loop(1, devices, drain, 0)


def tile_cross(devices, raw, fir, keep):
    rows = raw.shape[0] * raw.shape[1]
    dma = pltpu.SemaphoreType.DMA
    vmem = pl.BlockSpec(memory_space=pltpu.VMEM)
    hbm = pl.BlockSpec(memory_space=pltpu.HBM)
    line = pltpu.VMEM((WINDOWS, 1, SEG), jnp.float32)
    return pl.pallas_call(
        functools.partial(tile_kernel, devices),
        out_shape=pltpu.VMEM((TILE * STRIDE, TILE), jnp.float32),
        in_specs=[hbm] * 4,
        out_specs=vmem,
        scratch_shapes=[
            pltpu.VMEM(raw.shape, jnp.bfloat16), pltpu.VMEM((1, TAPS), jnp.float32),
            pltpu.VMEM(keep.shape[::-1], jnp.int32), pltpu.VMEM((2 * SEG, 2 * NBIN), jnp.bfloat16), dma((4,)),
            line, pltpu.VMEM((devices, 1, SEG), jnp.float32), line,
            pltpu.VMEM((devices, PIECES, rows, 2 * NBIN // PIECES), jnp.bfloat16),
            pltpu.VMEM((2 * WINDOWS * NBIN // PIECES, TILE), jnp.float32),
            dma((WINDOWS,)), dma((devices,)), dma((devices,)), dma((WINDOWS,)),
            dma((4, PIECES)), dma((4, PIECES)), dma((4, 2, PIECES)), dma((devices, PIECES)),
        ],
        compiler_params=pltpu.CompilerParams(
            collective_id=0, has_side_effects=True, vmem_limit_bytes=10 << 20
        ),
    )(*[pltpu.with_memory_space_constraint(x, pltpu.HBM) for x in (raw, fir.reshape(1, TAPS), keep.T, piece_tables())])


def lag_kernel(per_step, cross_ref, lag_ref, out_ref):
    base = pl.program_id(0) * per_step
    for group in range(per_step // 4):
        picked = []
        for member in range(4):
            start = (base + group * 4 + member) * STRIDE
            picked.append(cross_ref[pl.ds(start, 2 * NBIN), :].astype(jnp.bfloat16))
        stacked = contract(jnp.concatenate(picked, 1), lag_ref[...], 0, 0)
        out_ref[group * 4 : group * 4 + 4] = stacked.reshape(4, TILE, LAGS).astype(jnp.bfloat16)


def tile_stack(cross):
    per_step = 32
    vmem = pl.BlockSpec(memory_space=pltpu.VMEM)
    return pl.pallas_call(
        functools.partial(lag_kernel, per_step),
        out_shape=jax.ShapeDtypeStruct((TILE, TILE, LAGS), jnp.bfloat16),
        grid=(TILE // per_step,),
        in_specs=[vmem, vmem],
        out_specs=pl.BlockSpec((per_step, TILE, LAGS), lambda s: (s, 0, 0)),
        compiler_params=pltpu.CompilerParams(vmem_limit_bytes=12 << 20),
        cost_estimate=pl.CostEstimate(flops=5 << 30, bytes_accessed=12 << 20, transcendentals=0),
    )(cross, lag_table())


def local(raw, fir, keep, table):
    devices = lax.axis_size("tiles")
    if devices == WINDOWS and devices * raw.shape[1] == TILE:
        return tile_stack(tile_cross(devices, raw, fir, keep))[None]
    gathered = front(devices, raw, fir, keep)
    return stack(gathered, table)[None]


def solution(mesh):
    placed = (P(None, ("groups", "tiles"), None), P(), P(None, ("groups", "tiles")), P())
    return jax.shard_map(
        local,
        mesh=mesh,
        in_specs=placed,
        out_specs=P(("groups", "tiles"), None, None, None),
        check_vma=False,
    )
```

```python
import functools

import jax
import jax.numpy as jnp
import numpy as np
from jax import lax
from jax.experimental import pallas as pl
from jax.experimental.pallas import tpu as pltpu
from jax.sharding import PartitionSpec as P

WINDOWS = 16
TILE = 128
SEG = 512
LAGS = 256
TAPS = 64
DEC = 4
RAW = 2048
NBIN = 256
SPAN = 640
STRIDE = 521
PIECES = 4


def split2(x):
    high = x.astype(jnp.bfloat16)
    return high, (x - high.astype(jnp.float32)).astype(jnp.bfloat16)


def split3(x):
    high = x.astype(jnp.bfloat16)
    rest = x - high.astype(jnp.float32)
    middle = rest.astype(jnp.bfloat16)
    return high, middle, (rest - middle.astype(jnp.float32)).astype(jnp.bfloat16)


def contract(a, b, left, right):
    return lax.dot_general(a, b, (((left,), (right,)), ((), ())), preferred_element_type=jnp.float32)


def dft_tables():
    angle = 2.0 * np.pi / SEG * np.mod(np.arange(SEG)[:, None] * np.arange(NBIN)[None, :], SEG)
    table = np.concatenate([np.cos(angle), -np.sin(angle)], 1).astype(np.float32)
    high = table.astype(jnp.bfloat16)
    low = (table - high.astype(np.float32)).astype(jnp.bfloat16)
    return jnp.asarray(np.concatenate([high, low], 0))


def lag_table():
    freqs = np.arange(NBIN)
    shifts = np.arange(LAGS) - LAGS // 2
    angle = 2.0 * np.pi / SEG * np.mod(freqs[:, None] * shifts[None, :], SEG)
    weight = np.where(freqs == 0, 1.0, 2.0)[:, None] / np.sqrt(WINDOWS * NBIN)
    table = np.concatenate([weight * np.cos(angle), -weight * np.sin(angle)], 0)
    return jnp.asarray(table.astype(np.float32).astype(jnp.bfloat16))


def filter_rows(raw_ref, taps_ref):
    rows = raw_ref.shape[0] * raw_ref.shape[1]
    raw = raw_ref[...].astype(jnp.float32).reshape(rows, RAW).astype(jnp.bfloat16)
    taps = jnp.broadcast_to(taps_ref[...], (8, TAPS))
    places = lax.broadcasted_iota(jnp.int32, (TAPS, SPAN), 0) + lax.broadcasted_iota(jnp.int32, (TAPS, SPAN), 1)
    pick = jnp.where(places == TILE, 1.0, 0.0).astype(jnp.bfloat16)
    spread = sum(contract(part, pick, 1, 0) for part in split3(taps)[::-1])
    band = jnp.broadcast_to(spread[:1], (TILE, SPAN))
    index = lax.broadcasted_iota(jnp.int32, (TILE, SPAN), 0)
    for bit in range(7):
        band = jnp.where((index >> bit) & 1 == 1, pltpu.roll(band, DEC << bit, 1), band)
    pieces = [jnp.concatenate([jnp.zeros((rows, TILE), jnp.bfloat16), raw[:, :SEG]], 1)]
    for block in range(1, RAW // SEG):
        pieces.append(raw[:, block * SEG - TILE : (block + 1) * SEG])
    spans = jnp.concatenate(pieces, 0)
    out = sum(contract(spans, part, 1, 1) for part in split3(band)[::-1])
    return jnp.concatenate([out[b * rows : (b + 1) * rows] for b in range(RAW // SEG)], 1)


def whiten_rows(decimated, keep, table_ref):
    high, low = split2(decimated)
    table_high = table_ref[:SEG, :]
    spectrum = contract(low, table_high, 1, 0) + contract(high, table_ref[SEG:, :], 1, 0)
    spectrum = spectrum + contract(high, table_high, 1, 0)
    real_part, imag_part = spectrum[:, :NBIN], spectrum[:, NBIN:]
    power = real_part * real_part + imag_part * imag_part
    level = jnp.mean(power, -1, keepdims=True)
    scale = keep.astype(jnp.float32) * lax.rsqrt(0.5 * power + 0.5 * level + 1e-05)
    return jnp.concatenate([real_part * scale, imag_part * scale], 1).astype(jnp.bfloat16)


def arrange(piece_ref, spectra_ref):
    members, rows = piece_ref.shape[:2]
    width = rows // WINDOWS
    for pair in range(WINDOWS // 2):
        for quarter in range(4):
            block = piece_ref[:, pair * 2 * width : (pair + 1) * 2 * width, quarter * 128 : (quarter + 1) * 128]
            block = block.astype(jnp.float32)
            for half in range(2):
                turned = block[:, half * width : (half + 1) * width].reshape(members * width, 128).T
                start = (quarter % 2) * 128 * 32 + (quarter // 2) * WINDOWS + pair * 2 + half
                spectra_ref[pl.ds(start, 128, 32), :] = turned


def stack_kernel(same, per_step, *refs):
    if same:
        rows_ref, lag_ref, out_ref, cross_ref, row_spec = refs
    else:
        _, rows_ref, cols_ref, lag_ref, out_ref, cross_ref, row_spec, col_spec = refs

    @pl.when(pl.program_id(0) == 0)
    def _():
        arrange(rows_ref, row_spec)
        if not same:
            arrange(cols_ref, col_spec)

        def one_bin(f, carry):
            start = pl.multiple_of(f * 32, 32)
            left = row_spec[pl.ds(start, 32), :]
            right = left if same else col_spec[pl.ds(start, 32), :]
            turned = jnp.concatenate([right[WINDOWS:], -right[:WINDOWS]], 0)
            both = jnp.concatenate([right, turned], 1).astype(jnp.bfloat16)
            cross = contract(left.astype(jnp.bfloat16), both, 0, 0)
            cross_ref[pl.ds(f, TILE, STRIDE), :] = cross[:, :TILE]
            cross_ref[pl.ds(f + NBIN, TILE, STRIDE), :] = cross[:, TILE:]
            return carry

        lax.fori_loop(0, NBIN, one_bin, 0, unroll=64)

    base = pl.program_id(0) * per_step
    for group in range(per_step // 4):
        picked = []
        for member in range(4):
            start = (base + group * 4 + member) * STRIDE
            picked.append(cross_ref[pl.ds(start, 2 * NBIN), :].astype(jnp.bfloat16))
        stacked = contract(jnp.concatenate(picked, 1), lag_ref[...], 0, 0)
        out_ref[group * 4 : group * 4 + 4] = stacked.reshape(4, TILE, LAGS).astype(jnp.bfloat16)


def stack(gathered, table):
    members = TILE * WINDOWS // gathered.shape[1]
    same = gathered.shape[0] == members
    per_step = 32
    block = (members,) + gathered.shape[1:]
    spectra = pltpu.VMEM((2 * NBIN * WINDOWS, TILE), jnp.float32)
    if same:
        prefetch = []
        sides = [pl.BlockSpec(block, lambda s: (0, 0, 0))]
    else:
        prefetch = [table[lax.axis_index("tiles")]]
        sides = [
            pl.BlockSpec(block, lambda s, entry: (entry[0], 0, 0)),
            pl.BlockSpec(block, lambda s, entry: (entry[1], 0, 0)),
        ]
    return pl.pallas_call(
        functools.partial(stack_kernel, same, per_step),
        out_shape=jax.ShapeDtypeStruct((TILE, TILE, LAGS), jnp.bfloat16),
        grid_spec=pltpu.PrefetchScalarGridSpec(
            num_scalar_prefetch=len(prefetch),
            grid=(TILE // per_step,),
            in_specs=sides + [pl.BlockSpec((2 * NBIN, LAGS), lambda s, *entry: (0, 0))],
            out_specs=pl.BlockSpec((per_step, TILE, LAGS), lambda s, *entry: (s, 0, 0)),
            scratch_shapes=[pltpu.VMEM((TILE * STRIDE, TILE), jnp.float32)] + [spectra] * len(sides),
        ),
        compiler_params=pltpu.CompilerParams(vmem_limit_bytes=60 << 20),
        cost_estimate=pl.CostEstimate(flops=10 << 30, bytes_accessed=12 << 20, transcendentals=0),
    )(*prefetch, *[gathered] * len(sides), lag_table())


def other_core(me):
    return me + 1 - 2 * (me % 2)


def other_chip(me):
    return me + 2 - 4 * ((me // 2) % 2)


def remote(source, target, send, receive, peer):
    return pltpu.make_async_remote_copy(
        src_ref=source,
        dst_ref=target,
        send_sem=send,
        recv_sem=receive,
        device_id={"tiles": peer},
        device_id_type=pl.DeviceIdType.MESH,
    )


def front_kernel(
    devices, raw_hbm, taps_ref, keep_ref, table_hbm, out_ref,
    raw_ref, table_ref, load_sem, sum_buf, part_buf, common_buf, held,
    part_send, part_recv, common_send, common_recv,
    right_send, left_send, chip_send, core_send, held_recv, local_sem,
):
    me = lax.axis_index("tiles")
    channels = raw_ref.shape[1]
    rows = WINDOWS * channels
    barrier = pltpu.get_barrier_semaphore()
    all_owners = devices == WINDOWS

    def greet(k, carry):
        pl.semaphore_signal(
            barrier, inc=1, device_id={"tiles": (me + k) % devices}, device_id_type=pl.DeviceIdType.MESH
        )
        return carry

    lax.fori_loop(1, devices, greet, 0)
    load_raw = pltpu.make_async_copy(raw_hbm, raw_ref, load_sem.at[0])
    load_raw.start()
    load_table = pltpu.make_async_copy(table_hbm, table_ref, load_sem.at[1])
    load_table.start()
    load_raw.wait()
    filtered = filter_rows(raw_ref, taps_ref).reshape(WINDOWS, channels, SEG)
    sum_buf[...] = jnp.sum(filtered, 1, keepdims=True)
    pl.semaphore_wait(barrier, devices - 1)

    def part_copy(owner, slot):
        return remote(sum_buf.at[owner], part_buf.at[slot], part_send.at[owner], part_recv.at[slot], owner)

    def common_copy(owner, peer):
        return remote(common_buf.at[owner], common_buf.at[owner], common_send.at[peer], common_recv.at[owner], peer)

    def send_part(k, carry):
        owner = (me + k) % WINDOWS

        @pl.when(owner != me)
        def _():
            part_copy(owner, me).start()

        return carry

    lax.fori_loop(1 if all_owners else 0, WINDOWS, send_part, 0)

    @pl.when(me < WINDOWS)
    def _():
        part_buf[me] = sum_buf[me]

        def take(k, carry):
            part_copy(me, (me + k) % devices).wait_recv()
            return carry

        lax.fori_loop(1, devices, take, 0)
        common_buf[me] = jnp.sum(part_buf[...], 0)

        def give(k, carry):
            common_copy(me, (me + k) % devices).start()
            return carry

        lax.fori_loop(1, devices, give, 0)

    def take_common(k, carry):
        owner = (me + k) % WINDOWS

        @pl.when(owner != me)
        def _():
            common_copy(owner, me).wait_recv()

        return carry

    lax.fori_loop(1 if all_owners else 0, WINDOWS, take_common, 0)
    common = common_buf[...] / (channels * devices)
    decimated = (filtered - common).reshape(rows, SEG)
    keep = jnp.broadcast_to(keep_ref[...].astype(jnp.float32).T[:, :, None], (WINDOWS, channels, NBIN))
    load_table.wait()
    whitened = whiten_rows(decimated, keep.reshape(rows, NBIN), table_ref)
    held[me] = whitened.reshape(PIECES, rows // PIECES, 2 * NBIN)

    depth = devices // 4
    q, low = me // 4, me % 4
    chip, core = other_chip(me), other_core(me)

    def block_copy(block, piece, send, peer):
        return remote(held.at[block, piece], held.at[block, piece], send, held_recv.at[block, piece], peer)

    def to_right(level, piece):
        return block_copy(4 * level + low, piece, right_send.at[level, piece], (me + 4) % devices)

    def to_left(level, piece):
        return block_copy(4 * level + low, piece, left_send.at[level, piece], (me + devices - 4) % devices)

    def to_chip(level, piece):
        return block_copy(4 * level + low, piece, chip_send.at[level, piece], chip)

    def to_core(block, piece):
        return block_copy(block, piece, core_send.at[block // 2, piece], core)

    def local_copy(block, piece):
        part = rows // PIECES
        return pltpu.make_async_copy(
            held.at[block, piece], out_ref.at[block, pl.ds(piece * part, part)], local_sem.at[block, piece]
        )

    def arrived(block, piece):
        to_core(block, piece).wait_recv()
        local_copy(block, piece).start()

    def line_block(level, piece, forward, go):
        block = 4 * level + low
        arrived(block, piece)

        @pl.when(go)
        def _():
            forward(level, piece).start()

        to_chip(level, piece).start()
        to_core(block, piece).start()

    def chip_block(level, piece):
        block = 4 * level + other_chip(low)
        arrived(block, piece)
        to_core(block, piece).start()

    for piece in range(PIECES):
        @pl.when(q < depth - 1)
        def _():
            to_right(q, piece).start()

        @pl.when(q > 0)
        def _():
            to_left(q, piece).start()

        to_chip(q, piece).start()

    for piece in range(PIECES):
        to_core(me, piece).start()
        local_copy(me, piece).start()

    def step(d, carry):
        for piece in range(PIECES):
            @pl.when(q - d >= 0)
            def _():
                line_block(q - d, piece, to_right, q < depth - 1)

            @pl.when(q + d < depth)
            def _():
                line_block(q + d, piece, to_left, q > 0)

        for piece in range(PIECES):
            @pl.when(d == 1)
            def _():
                chip_block(q, piece)

            @pl.when((d > 1) & (q - d + 1 >= 0))
            def _():
                chip_block(q - d + 1, piece)

            @pl.when((d > 1) & (q + d - 1 < depth))
            def _():
                chip_block(q + d - 1, piece)

        return carry

    lax.fori_loop(1, depth + 1, step, 0)

    def from_core(pair, carry):
        for piece in range(PIECES):
            arrived(2 * pair + core % 2, piece)
        return carry

    lax.fori_loop(0, 2 * depth, from_core, 0)

    def finish(level, carry):
        for piece in range(PIECES):
            @pl.when((level <= q) & (q < depth - 1))
            def _():
                to_right(level, piece).wait_send()

            @pl.when((level >= q) & (q > 0))
            def _():
                to_left(level, piece).wait_send()

            to_chip(level, piece).wait_send()
            to_core(4 * level + low, piece).wait_send()
            to_core(4 * level + other_chip(low), piece).wait_send()
        return carry

    lax.fori_loop(0, depth, finish, 0)

    def drain_part(k, carry):
        owner = (me + k) % WINDOWS

        @pl.when(owner != me)
        def _():
            part_copy(owner, me).wait_send()

        return carry

    lax.fori_loop(1 if all_owners else 0, WINDOWS, drain_part, 0)

    @pl.when(me < WINDOWS)
    def _():
        def drain(k, carry):
            common_copy(me, (me + k) % devices).wait_send()
            return carry

        lax.fori_loop(1, devices, drain, 0)

    def settle(block, carry):
        for piece in range(PIECES):
            local_copy(block, piece).wait()
        return carry

    lax.fori_loop(0, devices, settle, 0)


def front(devices, raw, fir, keep):
    rows = raw.shape[0] * raw.shape[1]
    depth = devices // 4
    dma = pltpu.SemaphoreType.DMA
    vmem = pl.BlockSpec(memory_space=pltpu.VMEM)
    hbm = pl.BlockSpec(memory_space=pl.ANY)
    line = pltpu.VMEM((WINDOWS, 1, SEG), jnp.float32)
    return pl.pallas_call(
        functools.partial(front_kernel, devices),
        out_shape=jax.ShapeDtypeStruct((devices, rows, 2 * NBIN), jnp.bfloat16),
        in_specs=[hbm, vmem, vmem, hbm],
        out_specs=pl.BlockSpec(memory_space=pl.ANY),
        scratch_shapes=[
            pltpu.VMEM(raw.shape, jnp.bfloat16), pltpu.VMEM((2 * SEG, 2 * NBIN), jnp.bfloat16), dma((2,)),
            line, pltpu.VMEM((devices, 1, SEG), jnp.float32), line,
            pltpu.VMEM((devices, PIECES, rows // PIECES, 2 * NBIN), jnp.bfloat16),
            dma((WINDOWS,)), dma((devices,)), dma((devices,)), dma((WINDOWS,)),
            dma((depth, PIECES)), dma((depth, PIECES)), dma((depth, PIECES)), dma((2 * depth, PIECES)),
            dma((devices, PIECES)), dma((devices, PIECES)),
        ],
        compiler_params=pltpu.CompilerParams(
            collective_id=0, has_side_effects=True, vmem_limit_bytes=60 << 20
        ),
    )(raw, fir.reshape(1, TAPS), keep.T, dft_tables())


def piece_tables():
    angle = 2.0 * np.pi / SEG * np.mod(np.arange(SEG)[:, None] * np.arange(NBIN)[None, :], SEG)
    bins = NBIN // PIECES
    cosine, sine = np.cos(angle).reshape(SEG, PIECES, bins), -np.sin(angle).reshape(SEG, PIECES, bins)
    table = np.concatenate([cosine, sine], 2).reshape(SEG, 2 * NBIN).astype(np.float32)
    high = table.astype(jnp.bfloat16)
    low = (table - high.astype(np.float32)).astype(jnp.bfloat16)
    return jnp.asarray(np.concatenate([high, low], 0))


def whiten_pieces(decimated, keep, table_ref):
    high, low = split2(decimated)
    table_high = table_ref[:SEG, :]
    spectrum = contract(low, table_high, 1, 0) + contract(high, table_ref[SEG:, :], 1, 0)
    spectrum = spectrum + contract(high, table_high, 1, 0)
    width = 2 * NBIN // PIECES
    parts = [spectrum[:, p * width : (p + 1) * width] for p in range(PIECES)]
    squares = [part * part for part in parts]
    level = jnp.sum(sum(squares), -1, keepdims=True) / NBIN
    whitened = []
    for part, square in zip(parts, squares):
        power = square + pltpu.roll(square, width // 2, 1)
        scale = keep * lax.rsqrt(0.5 * power + 0.5 * level + 1e-05)
        whitened.append((part * scale).astype(jnp.bfloat16))
    return whitened


PITCH = 33


def tile_kernel(
    devices, raw_hbm, taps_hbm, keep_hbm, table_hbm, cross_ref,
    raw_ref, taps_ref, keep_ref, table_ref, load_sem,
    sum_buf, pair_buf, chip_buf, common_buf, held, spectra_ref,
    pair_send, pair_recv, sum_send, sum_recv, common_send, common_recv,
    right_send, left_send, chip_send, core_send, held_recv,
):
    me = lax.axis_index("tiles")
    channels = raw_ref.shape[1]
    rows = WINDOWS * channels
    chips = devices // 2
    here, core = me // 2, me % 2
    partner = 2 * here + 1 - core
    barrier = pltpu.get_barrier_semaphore()

    def greet(device):
        pl.semaphore_signal(
            barrier, inc=1, device_id={"tiles": device}, device_id_type=pl.DeviceIdType.MESH
        )

    greet(partner)
    for k in range(1, chips):
        greet(2 * ((here + k) % chips) + core)
    load_raw = pltpu.make_async_copy(raw_hbm, raw_ref, load_sem.at[0])
    load_raw.start()
    load_taps = pltpu.make_async_copy(taps_hbm, taps_ref, load_sem.at[2])
    load_taps.start()
    load_keep = pltpu.make_async_copy(keep_hbm, keep_ref, load_sem.at[3])
    load_keep.start()
    load_table = pltpu.make_async_copy(table_hbm, table_ref, load_sem.at[1])
    load_table.start()
    load_taps.wait()
    load_raw.wait()
    filtered = filter_rows(raw_ref, taps_ref).reshape(WINDOWS, channels, SEG)
    sum_buf[...] = jnp.sum(filtered, 1).reshape(sum_buf.shape)
    pl.semaphore_wait(barrier, chips)

    pair = remote(sum_buf.at[1 - core], pair_buf, pair_send, pair_recv, partner)
    pair.start()
    pair.wait_recv()
    chip_buf[here] = sum_buf[core] + pair_buf[...]

    def sum_copy(chip, k):
        return remote(
            chip_buf.at[chip], chip_buf.at[chip], sum_send.at[k], sum_recv.at[chip], 2 * ((here + k) % chips) + core
        )

    for k in range(1, chips):
        sum_copy(here, k).start()
    for k in range(1, chips):
        sum_copy((here + k) % chips, k).wait_recv()
    common_buf[core] = jnp.sum(chip_buf[...], 0)

    def common_copy(half):
        return remote(common_buf.at[half], common_buf.at[half], common_send, common_recv, partner)

    common_copy(core).start()
    common_copy(1 - core).wait_recv()
    common = common_buf[...].reshape(WINDOWS, 1, SEG) / (channels * devices)
    decimated = (filtered - common).reshape(rows, SEG)
    load_keep.wait()
    keep = jnp.broadcast_to(keep_ref[...].astype(jnp.float32).T[:, :, None], (WINDOWS, channels, 128))
    load_table.wait()
    whitened = whiten_pieces(decimated, keep.reshape(rows, 128), table_ref)
    for piece in range(PIECES):
        held[me, piece] = whitened[piece]

    level, chip = me // 4, (me // 2) % 2
    last = devices // 4 - 1

    def at(line, chip_off, core_off):
        return 4 * line + 2 * (chip + chip_off - 2 * chip * chip_off) + core + core_off - 2 * core * core_off

    def block_copy(block, piece, send, peer):
        return remote(held.at[block, piece], held.at[block, piece], send, held_recv.at[block, piece], peer)

    def to_right(line, piece):
        return block_copy(at(line, 0, 0), piece, right_send.at[line, piece], (me + 4) % devices)

    def to_left(line, piece):
        return block_copy(at(line, 0, 0), piece, left_send.at[line, piece], (me + devices - 4) % devices)

    def to_chip(line, piece):
        return block_copy(at(line, 0, 0), piece, chip_send.at[line, piece], at(level, 1, 0))

    def to_core(line, chip_off, piece):
        return block_copy(at(line, chip_off, 0), piece, core_send.at[line, chip_off, piece], at(level, 0, 1))

    def arrived(line, chip_off, core_off, piece):
        block = at(line, chip_off, core_off)
        block_copy(block, piece, held_recv.at[block, piece], partner).wait_recv()

    def sides(d, action):
        pl.when(level >= d)(lambda: action(level - d, 1))
        pl.when(level + d <= last)(lambda: action(level + d, -1))

    def own(piece):
        pl.when(level < last)(lambda: to_right(level, piece).start())
        pl.when(level > 0)(lambda: to_left(level, piece).start())
        to_chip(level, piece).start()
        to_core(level, 0, piece).start()

    def line_step(d, piece):
        def take(line, sign):
            arrived(line, 0, 0, piece)
            if d < last:
                if sign > 0:
                    pl.when(level < last)(lambda: to_right(line, piece).start())
                else:
                    pl.when(level > 0)(lambda: to_left(line, piece).start())
            to_chip(line, piece).start()
            to_core(line, 0, piece).start()

        sides(d, take)

    def chip_step(d, piece):
        def take(line, sign):
            arrived(line, 1, 0, piece)
            to_core(line, 1, piece).start()

        if d == 0:
            take(level, 0)
        else:
            sides(d, take)

    def core_step(piece):
        for chip_off in range(2):
            for line in range(last + 1):
                arrived(line, chip_off, 1, piece)

    bins = NBIN // PIECES

    def turn(piece):
        for pair in range(WINDOWS // 2):
            block = held[:, piece, pair * 2 * channels : (pair + 1) * 2 * channels, :].astype(jnp.float32)
            for half in range(2):
                turned = block[:, half * channels : (half + 1) * channels].reshape(devices * channels, 2 * bins).T
                window = pair * 2 + half
                spectra_ref[piece % 2, pl.ds(window, bins, PITCH), :] = turned[:bins]
                spectra_ref[piece % 2, pl.ds(WINDOWS + window, bins, PITCH), :] = turned[bins:]

    def multiply(piece):
        place = lax.broadcasted_iota(jnp.int32, (TILE, 8 * 2 * WINDOWS), 1) // (2 * WINDOWS)

        def eight_bins(g):
            spans = [spectra_ref[piece % 2, pl.ds((g * 8 + k) * PITCH, 2 * WINDOWS), :] for k in range(8)]
            right = jnp.concatenate(spans, 0)
            split = right.reshape(8, 2, WINDOWS, TILE)
            turned = jnp.concatenate([split[:, 1:], -split[:, :1]], 1).reshape(16 * WINDOWS, TILE)
            both = jnp.concatenate([right, turned], 1).astype(jnp.bfloat16)
            left = right.T
            picked = [jnp.where(place == k, left, 0.0).astype(jnp.bfloat16) for k in range(8)]
            cross = contract(jnp.concatenate(picked, 0), both, 1, 0)
            for k in range(8):
                f = piece * bins + g * 8 + k
                cross_ref[pl.ds(f, TILE, STRIDE), :] = cross[k * TILE : (k + 1) * TILE, :TILE]
                cross_ref[pl.ds(f + NBIN, TILE, STRIDE), :] = cross[k * TILE : (k + 1) * TILE, TILE:]

        for g in range(bins // 8):
            eight_bins(g)

    for piece in range(PIECES):
        own(piece)
    for d in range(1, last + 1):
        for piece in range(PIECES):
            line_step(d, piece)
        for piece in range(PIECES):
            chip_step(d - 1, piece)
    chip_step(last, 0)
    chip_step(last, 1)
    core_step(0)
    turn(0)
    chip_step(last, 2)
    chip_step(last, 3)
    core_step(1)
    turn(1)
    multiply(0)
    core_step(2)
    core_step(3)
    turn(2)
    multiply(1)
    turn(3)
    multiply(2)
    multiply(3)

    for piece in range(PIECES):
        pl.when(level < last)(lambda: to_right(level, piece).wait_send())
        pl.when(level > 0)(lambda: to_left(level, piece).wait_send())
        to_chip(level, piece).wait_send()
        to_core(level, 0, piece).wait_send()
        to_core(level, 1, piece).wait_send()
        for d in range(1, last + 1):
            def drain(line, sign):
                if d < last:
                    if sign > 0:
                        pl.when(level < last)(lambda: to_right(line, piece).wait_send())
                    else:
                        pl.when(level > 0)(lambda: to_left(line, piece).wait_send())
                to_chip(line, piece).wait_send()
                to_core(line, 0, piece).wait_send()
                to_core(line, 1, piece).wait_send()

            sides(d, drain)

    pair.wait_send()
    common_copy(core).wait_send()
    for k in range(1, chips):
        sum_copy(here, k).wait_send()


def tile_cross(devices, raw, fir, keep):
    rows = raw.shape[0] * raw.shape[1]
    dma = pltpu.SemaphoreType.DMA
    vmem = pl.BlockSpec(memory_space=pltpu.VMEM)
    hbm = pl.BlockSpec(memory_space=pltpu.HBM)
    half = (2, WINDOWS // 2, SEG)
    return pl.pallas_call(
        functools.partial(tile_kernel, devices),
        out_shape=pltpu.VMEM((TILE * STRIDE, TILE), jnp.float32),
        in_specs=[hbm] * 4,
        out_specs=vmem,
        scratch_shapes=[
            pltpu.VMEM(raw.shape, jnp.bfloat16), pltpu.VMEM((1, TAPS), jnp.float32),
            pltpu.VMEM(keep.shape[::-1], jnp.int32), pltpu.VMEM((2 * SEG, 2 * NBIN), jnp.bfloat16), dma((4,)),
            pltpu.VMEM(half, jnp.float32), pltpu.VMEM(half[1:], jnp.float32),
            pltpu.VMEM((devices // 2,) + half[1:], jnp.float32), pltpu.VMEM(half, jnp.float32),
            pltpu.VMEM((devices, PIECES, rows, 2 * NBIN // PIECES), jnp.bfloat16),
            pltpu.VMEM((2, PITCH * NBIN // PIECES, TILE), jnp.float32),
            dma, dma, dma((devices // 2,)), dma((devices // 2,)), dma, dma,
            dma((4, PIECES)), dma((4, PIECES)), dma((4, PIECES)), dma((4, 2, PIECES)), dma((devices, PIECES)),
        ],
        compiler_params=pltpu.CompilerParams(
            collective_id=0, has_side_effects=True, vmem_limit_bytes=10 << 20
        ),
    )(*[pltpu.with_memory_space_constraint(x, pltpu.HBM) for x in (raw, fir.reshape(1, TAPS), keep.T, piece_tables())])


def lag_kernel(per_step, cross_ref, lag_ref, out_ref):
    base = pl.program_id(0) * per_step
    for group in range(per_step // 4):
        picked = []
        for member in range(4):
            start = (base + group * 4 + member) * STRIDE
            picked.append(cross_ref[pl.ds(start, 2 * NBIN), :].astype(jnp.bfloat16))
        stacked = contract(jnp.concatenate(picked, 1), lag_ref[...], 0, 0)
        out_ref[group * 4 : group * 4 + 4] = stacked.reshape(4, TILE, LAGS).astype(jnp.bfloat16)


def tile_stack(cross):
    per_step = 32
    vmem = pl.BlockSpec(memory_space=pltpu.VMEM)
    return pl.pallas_call(
        functools.partial(lag_kernel, per_step),
        out_shape=jax.ShapeDtypeStruct((TILE, TILE, LAGS), jnp.bfloat16),
        grid=(TILE // per_step,),
        in_specs=[vmem, vmem],
        out_specs=pl.BlockSpec((per_step, TILE, LAGS), lambda s: (s, 0, 0)),
        compiler_params=pltpu.CompilerParams(vmem_limit_bytes=12 << 20),
        cost_estimate=pl.CostEstimate(flops=5 << 30, bytes_accessed=12 << 20, transcendentals=0),
    )(cross, lag_table())


def local(raw, fir, keep, table):
    devices = lax.axis_size("tiles")
    if devices == WINDOWS and devices * raw.shape[1] == TILE:
        return tile_stack(tile_cross(devices, raw, fir, keep))[None]
    gathered = front(devices, raw, fir, keep)
    return stack(gathered, table)[None]


def solution(mesh):
    placed = (P(None, ("groups", "tiles"), None), P(), P(None, ("groups", "tiles")), P())
    return jax.shard_map(
        local,
        mesh=mesh,
        in_specs=placed,
        out_specs=P(("groups", "tiles"), None, None, None),
        check_vma=False,
    )
```

```python
import functools

import jax
import jax.numpy as jnp
import numpy as np
from jax import lax
from jax.experimental import pallas as pl
from jax.experimental.pallas import tpu as pltpu
from jax.sharding import PartitionSpec as P

WINDOWS = 16
TILE = 128
SEG = 512
LAGS = 256
TAPS = 64
DEC = 4
RAW = 2048
NBIN = 256
SPAN = 640
STRIDE = 521
PIECES = 4


def split2(x):
    high = x.astype(jnp.bfloat16)
    return high, (x - high.astype(jnp.float32)).astype(jnp.bfloat16)


def split3(x):
    high = x.astype(jnp.bfloat16)
    rest = x - high.astype(jnp.float32)
    middle = rest.astype(jnp.bfloat16)
    return high, middle, (rest - middle.astype(jnp.float32)).astype(jnp.bfloat16)


def contract(a, b, left, right):
    return lax.dot_general(a, b, (((left,), (right,)), ((), ())), preferred_element_type=jnp.float32)


def dft_tables():
    angle = 2.0 * np.pi / SEG * np.mod(np.arange(SEG)[:, None] * np.arange(NBIN)[None, :], SEG)
    table = np.concatenate([np.cos(angle), -np.sin(angle)], 1).astype(np.float32)
    high = table.astype(jnp.bfloat16)
    low = (table - high.astype(np.float32)).astype(jnp.bfloat16)
    return jnp.asarray(np.concatenate([high, low], 0))


def lag_table():
    freqs = np.arange(NBIN)
    shifts = np.arange(LAGS) - LAGS // 2
    angle = 2.0 * np.pi / SEG * np.mod(freqs[:, None] * shifts[None, :], SEG)
    weight = np.where(freqs == 0, 1.0, 2.0)[:, None] / np.sqrt(WINDOWS * NBIN)
    table = np.concatenate([weight * np.cos(angle), -weight * np.sin(angle)], 0)
    return jnp.asarray(table.astype(np.float32).astype(jnp.bfloat16))


def filter_rows(raw_ref, taps_ref):
    rows = raw_ref.shape[0] * raw_ref.shape[1]
    raw = raw_ref[...].astype(jnp.float32).reshape(rows, RAW).astype(jnp.bfloat16)
    taps = jnp.broadcast_to(taps_ref[...], (8, TAPS))
    places = lax.broadcasted_iota(jnp.int32, (TAPS, SPAN), 0) + lax.broadcasted_iota(jnp.int32, (TAPS, SPAN), 1)
    pick = jnp.where(places == TILE, 1.0, 0.0).astype(jnp.bfloat16)
    spread = sum(contract(part, pick, 1, 0) for part in split3(taps)[::-1])
    band = jnp.broadcast_to(spread[:1], (TILE, SPAN))
    index = lax.broadcasted_iota(jnp.int32, (TILE, SPAN), 0)
    for bit in range(7):
        band = jnp.where((index >> bit) & 1 == 1, pltpu.roll(band, DEC << bit, 1), band)
    pieces = [jnp.concatenate([jnp.zeros((rows, TILE), jnp.bfloat16), raw[:, :SEG]], 1)]
    for block in range(1, RAW // SEG):
        pieces.append(raw[:, block * SEG - TILE : (block + 1) * SEG])
    spans = jnp.concatenate(pieces, 0)
    out = sum(contract(spans, part, 1, 1) for part in split3(band)[::-1])
    return jnp.concatenate([out[b * rows : (b + 1) * rows] for b in range(RAW // SEG)], 1)


def whiten_rows(decimated, keep, table_ref):
    high, low = split2(decimated)
    table_high = table_ref[:SEG, :]
    spectrum = contract(low, table_high, 1, 0) + contract(high, table_ref[SEG:, :], 1, 0)
    spectrum = spectrum + contract(high, table_high, 1, 0)
    real_part, imag_part = spectrum[:, :NBIN], spectrum[:, NBIN:]
    power = real_part * real_part + imag_part * imag_part
    level = jnp.mean(power, -1, keepdims=True)
    scale = keep.astype(jnp.float32) * lax.rsqrt(0.5 * power + 0.5 * level + 1e-05)
    return jnp.concatenate([real_part * scale, imag_part * scale], 1).astype(jnp.bfloat16)


def arrange(piece_ref, spectra_ref):
    members, rows = piece_ref.shape[:2]
    width = rows // WINDOWS
    for pair in range(WINDOWS // 2):
        for quarter in range(4):
            block = piece_ref[:, pair * 2 * width : (pair + 1) * 2 * width, quarter * 128 : (quarter + 1) * 128]
            block = block.astype(jnp.float32)
            for half in range(2):
                turned = block[:, half * width : (half + 1) * width].reshape(members * width, 128).T
                start = (quarter % 2) * 128 * 32 + (quarter // 2) * WINDOWS + pair * 2 + half
                spectra_ref[pl.ds(start, 128, 32), :] = turned


def stack_kernel(same, per_step, *refs):
    if same:
        rows_ref, lag_ref, out_ref, cross_ref, row_spec = refs
    else:
        _, rows_ref, cols_ref, lag_ref, out_ref, cross_ref, row_spec, col_spec = refs

    @pl.when(pl.program_id(0) == 0)
    def _():
        arrange(rows_ref, row_spec)
        if not same:
            arrange(cols_ref, col_spec)

        def one_bin(f, carry):
            start = pl.multiple_of(f * 32, 32)
            left = row_spec[pl.ds(start, 32), :]
            right = left if same else col_spec[pl.ds(start, 32), :]
            turned = jnp.concatenate([right[WINDOWS:], -right[:WINDOWS]], 0)
            both = jnp.concatenate([right, turned], 1).astype(jnp.bfloat16)
            cross = contract(left.astype(jnp.bfloat16), both, 0, 0)
            cross_ref[pl.ds(f, TILE, STRIDE), :] = cross[:, :TILE]
            cross_ref[pl.ds(f + NBIN, TILE, STRIDE), :] = cross[:, TILE:]
            return carry

        lax.fori_loop(0, NBIN, one_bin, 0, unroll=64)

    base = pl.program_id(0) * per_step
    for group in range(per_step // 4):
        picked = []
        for member in range(4):
            start = (base + group * 4 + member) * STRIDE
            picked.append(cross_ref[pl.ds(start, 2 * NBIN), :].astype(jnp.bfloat16))
        stacked = contract(jnp.concatenate(picked, 1), lag_ref[...], 0, 0)
        out_ref[group * 4 : group * 4 + 4] = stacked.reshape(4, TILE, LAGS).astype(jnp.bfloat16)


def stack(gathered, table):
    members = TILE * WINDOWS // gathered.shape[1]
    same = gathered.shape[0] == members
    per_step = 32
    block = (members,) + gathered.shape[1:]
    spectra = pltpu.VMEM((2 * NBIN * WINDOWS, TILE), jnp.float32)
    if same:
        prefetch = []
        sides = [pl.BlockSpec(block, lambda s: (0, 0, 0))]
    else:
        prefetch = [table[lax.axis_index("tiles")]]
        sides = [
            pl.BlockSpec(block, lambda s, entry: (entry[0], 0, 0)),
            pl.BlockSpec(block, lambda s, entry: (entry[1], 0, 0)),
        ]
    return pl.pallas_call(
        functools.partial(stack_kernel, same, per_step),
        out_shape=jax.ShapeDtypeStruct((TILE, TILE, LAGS), jnp.bfloat16),
        grid_spec=pltpu.PrefetchScalarGridSpec(
            num_scalar_prefetch=len(prefetch),
            grid=(TILE // per_step,),
            in_specs=sides + [pl.BlockSpec((2 * NBIN, LAGS), lambda s, *entry: (0, 0))],
            out_specs=pl.BlockSpec((per_step, TILE, LAGS), lambda s, *entry: (s, 0, 0)),
            scratch_shapes=[pltpu.VMEM((TILE * STRIDE, TILE), jnp.float32)] + [spectra] * len(sides),
        ),
        compiler_params=pltpu.CompilerParams(vmem_limit_bytes=60 << 20),
        cost_estimate=pl.CostEstimate(flops=10 << 30, bytes_accessed=12 << 20, transcendentals=0),
    )(*prefetch, *[gathered] * len(sides), lag_table())


def other_core(me):
    return me + 1 - 2 * (me % 2)


def other_chip(me):
    return me + 2 - 4 * ((me // 2) % 2)


def remote(source, target, send, receive, peer):
    return pltpu.make_async_remote_copy(
        src_ref=source,
        dst_ref=target,
        send_sem=send,
        recv_sem=receive,
        device_id={"tiles": peer},
        device_id_type=pl.DeviceIdType.MESH,
    )


def front_kernel(
    devices, raw_hbm, taps_ref, keep_ref, table_hbm, out_ref,
    raw_ref, table_ref, load_sem, sum_buf, part_buf, common_buf, held,
    part_send, part_recv, common_send, common_recv,
    right_send, left_send, chip_send, core_send, held_recv, local_sem,
):
    me = lax.axis_index("tiles")
    channels = raw_ref.shape[1]
    rows = WINDOWS * channels
    barrier = pltpu.get_barrier_semaphore()
    all_owners = devices == WINDOWS

    def greet(k, carry):
        pl.semaphore_signal(
            barrier, inc=1, device_id={"tiles": (me + k) % devices}, device_id_type=pl.DeviceIdType.MESH
        )
        return carry

    lax.fori_loop(1, devices, greet, 0)
    load_raw = pltpu.make_async_copy(raw_hbm, raw_ref, load_sem.at[0])
    load_raw.start()
    load_table = pltpu.make_async_copy(table_hbm, table_ref, load_sem.at[1])
    load_table.start()
    load_raw.wait()
    filtered = filter_rows(raw_ref, taps_ref).reshape(WINDOWS, channels, SEG)
    sum_buf[...] = jnp.sum(filtered, 1, keepdims=True)
    pl.semaphore_wait(barrier, devices - 1)

    def part_copy(owner, slot):
        return remote(sum_buf.at[owner], part_buf.at[slot], part_send.at[owner], part_recv.at[slot], owner)

    def common_copy(owner, peer):
        return remote(common_buf.at[owner], common_buf.at[owner], common_send.at[peer], common_recv.at[owner], peer)

    def send_part(k, carry):
        owner = (me + k) % WINDOWS

        @pl.when(owner != me)
        def _():
            part_copy(owner, me).start()

        return carry

    lax.fori_loop(1 if all_owners else 0, WINDOWS, send_part, 0)

    @pl.when(me < WINDOWS)
    def _():
        part_buf[me] = sum_buf[me]

        def take(k, carry):
            part_copy(me, (me + k) % devices).wait_recv()
            return carry

        lax.fori_loop(1, devices, take, 0)
        common_buf[me] = jnp.sum(part_buf[...], 0)

        def give(k, carry):
            common_copy(me, (me + k) % devices).start()
            return carry

        lax.fori_loop(1, devices, give, 0)

    def take_common(k, carry):
        owner = (me + k) % WINDOWS

        @pl.when(owner != me)
        def _():
            common_copy(owner, me).wait_recv()

        return carry

    lax.fori_loop(1 if all_owners else 0, WINDOWS, take_common, 0)
    common = common_buf[...] / (channels * devices)
    decimated = (filtered - common).reshape(rows, SEG)
    keep = jnp.broadcast_to(keep_ref[...].astype(jnp.float32).T[:, :, None], (WINDOWS, channels, NBIN))
    load_table.wait()
    whitened = whiten_rows(decimated, keep.reshape(rows, NBIN), table_ref)
    held[me] = whitened.reshape(PIECES, rows // PIECES, 2 * NBIN)

    depth = devices // 4
    q, low = me // 4, me % 4
    chip, core = other_chip(me), other_core(me)

    def block_copy(block, piece, send, peer):
        return remote(held.at[block, piece], held.at[block, piece], send, held_recv.at[block, piece], peer)

    def to_right(level, piece):
        return block_copy(4 * level + low, piece, right_send.at[level, piece], (me + 4) % devices)

    def to_left(level, piece):
        return block_copy(4 * level + low, piece, left_send.at[level, piece], (me + devices - 4) % devices)

    def to_chip(level, piece):
        return block_copy(4 * level + low, piece, chip_send.at[level, piece], chip)

    def to_core(block, piece):
        return block_copy(block, piece, core_send.at[block // 2, piece], core)

    def local_copy(block, piece):
        part = rows // PIECES
        return pltpu.make_async_copy(
            held.at[block, piece], out_ref.at[block, pl.ds(piece * part, part)], local_sem.at[block, piece]
        )

    def arrived(block, piece):
        to_core(block, piece).wait_recv()
        local_copy(block, piece).start()

    def line_block(level, piece, forward, go):
        block = 4 * level + low
        arrived(block, piece)

        @pl.when(go)
        def _():
            forward(level, piece).start()

        to_chip(level, piece).start()
        to_core(block, piece).start()

    def chip_block(level, piece):
        block = 4 * level + other_chip(low)
        arrived(block, piece)
        to_core(block, piece).start()

    for piece in range(PIECES):
        @pl.when(q < depth - 1)
        def _():
            to_right(q, piece).start()

        @pl.when(q > 0)
        def _():
            to_left(q, piece).start()

        to_chip(q, piece).start()

    for piece in range(PIECES):
        to_core(me, piece).start()
        local_copy(me, piece).start()

    def step(d, carry):
        for piece in range(PIECES):
            @pl.when(q - d >= 0)
            def _():
                line_block(q - d, piece, to_right, q < depth - 1)

            @pl.when(q + d < depth)
            def _():
                line_block(q + d, piece, to_left, q > 0)

        for piece in range(PIECES):
            @pl.when(d == 1)
            def _():
                chip_block(q, piece)

            @pl.when((d > 1) & (q - d + 1 >= 0))
            def _():
                chip_block(q - d + 1, piece)

            @pl.when((d > 1) & (q + d - 1 < depth))
            def _():
                chip_block(q + d - 1, piece)

        return carry

    lax.fori_loop(1, depth + 1, step, 0)

    def from_core(pair, carry):
        for piece in range(PIECES):
            arrived(2 * pair + core % 2, piece)
        return carry

    lax.fori_loop(0, 2 * depth, from_core, 0)

    def finish(level, carry):
        for piece in range(PIECES):
            @pl.when((level <= q) & (q < depth - 1))
            def _():
                to_right(level, piece).wait_send()

            @pl.when((level >= q) & (q > 0))
            def _():
                to_left(level, piece).wait_send()

            to_chip(level, piece).wait_send()
            to_core(4 * level + low, piece).wait_send()
            to_core(4 * level + other_chip(low), piece).wait_send()
        return carry

    lax.fori_loop(0, depth, finish, 0)

    def drain_part(k, carry):
        owner = (me + k) % WINDOWS

        @pl.when(owner != me)
        def _():
            part_copy(owner, me).wait_send()

        return carry

    lax.fori_loop(1 if all_owners else 0, WINDOWS, drain_part, 0)

    @pl.when(me < WINDOWS)
    def _():
        def drain(k, carry):
            common_copy(me, (me + k) % devices).wait_send()
            return carry

        lax.fori_loop(1, devices, drain, 0)

    def settle(block, carry):
        for piece in range(PIECES):
            local_copy(block, piece).wait()
        return carry

    lax.fori_loop(0, devices, settle, 0)


def front(devices, raw, fir, keep):
    rows = raw.shape[0] * raw.shape[1]
    depth = devices // 4
    dma = pltpu.SemaphoreType.DMA
    vmem = pl.BlockSpec(memory_space=pltpu.VMEM)
    hbm = pl.BlockSpec(memory_space=pl.ANY)
    line = pltpu.VMEM((WINDOWS, 1, SEG), jnp.float32)
    return pl.pallas_call(
        functools.partial(front_kernel, devices),
        out_shape=jax.ShapeDtypeStruct((devices, rows, 2 * NBIN), jnp.bfloat16),
        in_specs=[hbm, vmem, vmem, hbm],
        out_specs=pl.BlockSpec(memory_space=pl.ANY),
        scratch_shapes=[
            pltpu.VMEM(raw.shape, jnp.bfloat16), pltpu.VMEM((2 * SEG, 2 * NBIN), jnp.bfloat16), dma((2,)),
            line, pltpu.VMEM((devices, 1, SEG), jnp.float32), line,
            pltpu.VMEM((devices, PIECES, rows // PIECES, 2 * NBIN), jnp.bfloat16),
            dma((WINDOWS,)), dma((devices,)), dma((devices,)), dma((WINDOWS,)),
            dma((depth, PIECES)), dma((depth, PIECES)), dma((depth, PIECES)), dma((2 * depth, PIECES)),
            dma((devices, PIECES)), dma((devices, PIECES)),
        ],
        compiler_params=pltpu.CompilerParams(
            collective_id=0, has_side_effects=True, vmem_limit_bytes=60 << 20
        ),
    )(raw, fir.reshape(1, TAPS), keep.T, dft_tables())


def piece_tables():
    angle = 2.0 * np.pi / SEG * np.mod(np.arange(SEG)[:, None] * np.arange(NBIN)[None, :], SEG)
    bins = NBIN // PIECES
    cosine, sine = np.cos(angle).reshape(SEG, PIECES, bins), -np.sin(angle).reshape(SEG, PIECES, bins)
    table = np.concatenate([cosine, sine], 2).reshape(SEG, 2 * NBIN).astype(np.float32)
    high = table.astype(jnp.bfloat16)
    low = (table - high.astype(np.float32)).astype(jnp.bfloat16)
    return jnp.asarray(np.concatenate([high, low], 0))


def whiten_pieces(decimated, keep, table_ref):
    high, low = split2(decimated)
    table_high = table_ref[:SEG, :]
    spectrum = contract(low, table_high, 1, 0) + contract(high, table_ref[SEG:, :], 1, 0)
    spectrum = spectrum + contract(high, table_high, 1, 0)
    width = 2 * NBIN // PIECES
    parts = [spectrum[:, p * width : (p + 1) * width] for p in range(PIECES)]
    squares = [part * part for part in parts]
    level = jnp.sum(sum(squares), -1, keepdims=True) / NBIN
    whitened = []
    for part, square in zip(parts, squares):
        power = square + pltpu.roll(square, width // 2, 1)
        scale = keep * lax.rsqrt(0.5 * power + 0.5 * level + 1e-05)
        whitened.append((part * scale).astype(jnp.bfloat16))
    return whitened


PITCH = 33
HALF = TILE // 2
UPPER = HALF * STRIDE
NARROW = NBIN + 1
TURN = HALF + 1


def tile_kernel(
    devices, raw_hbm, taps_hbm, keep_hbm, table_hbm, cross_ref,
    raw_ref, taps_ref, keep_ref, table_ref, load_sem,
    sum_buf, pair_buf, chip_buf, common_buf, held, spectra_ref,
    pair_send, pair_recv, sum_send, sum_recv, common_send, common_recv,
    right_send, left_send, chip_send, core_send, held_recv,
):
    me = lax.axis_index("tiles")
    channels = raw_ref.shape[1]
    rows = WINDOWS * channels
    chips = devices // 2
    here, core = me // 2, me % 2
    partner = 2 * here + 1 - core
    barrier = pltpu.get_barrier_semaphore()

    def greet(device):
        pl.semaphore_signal(
            barrier, inc=1, device_id={"tiles": device}, device_id_type=pl.DeviceIdType.MESH
        )

    greet(partner)
    for k in range(1, chips):
        greet(2 * ((here + k) % chips) + core)
    load_raw = pltpu.make_async_copy(raw_hbm, raw_ref, load_sem.at[0])
    load_raw.start()
    load_taps = pltpu.make_async_copy(taps_hbm, taps_ref, load_sem.at[2])
    load_taps.start()
    load_keep = pltpu.make_async_copy(keep_hbm, keep_ref, load_sem.at[3])
    load_keep.start()
    load_table = pltpu.make_async_copy(table_hbm, table_ref, load_sem.at[1])
    load_table.start()
    load_taps.wait()
    load_raw.wait()
    filtered = filter_rows(raw_ref, taps_ref).reshape(WINDOWS, channels, SEG)
    sum_buf[...] = jnp.sum(filtered, 1).reshape(sum_buf.shape)
    pl.semaphore_wait(barrier, chips)

    pair = remote(sum_buf.at[1 - core], pair_buf, pair_send, pair_recv, partner)
    pair.start()
    pair.wait_recv()
    chip_buf[here] = sum_buf[core] + pair_buf[...]

    def sum_copy(chip, k):
        return remote(
            chip_buf.at[chip], chip_buf.at[chip], sum_send.at[k], sum_recv.at[chip], 2 * ((here + k) % chips) + core
        )

    for k in range(1, chips):
        sum_copy(here, k).start()
    for k in range(1, chips):
        sum_copy((here + k) % chips, k).wait_recv()
    common_buf[core] = jnp.sum(chip_buf[...], 0)

    def common_copy(half):
        return remote(common_buf.at[half], common_buf.at[half], common_send, common_recv, partner)

    common_copy(core).start()
    common_copy(1 - core).wait_recv()
    common = common_buf[...].reshape(WINDOWS, 1, SEG) / (channels * devices)
    decimated = (filtered - common).reshape(rows, SEG)
    load_keep.wait()
    keep = jnp.broadcast_to(keep_ref[...].astype(jnp.float32).T[:, :, None], (WINDOWS, channels, 128))
    load_table.wait()
    whitened = whiten_pieces(decimated, keep.reshape(rows, 128), table_ref)
    for piece in range(PIECES):
        held[me, piece] = whitened[piece]

    level, chip = me // 4, (me // 2) % 2
    last = devices // 4 - 1

    def at(line, chip_off, core_off):
        return 4 * line + 2 * (chip + chip_off - 2 * chip * chip_off) + core + core_off - 2 * core * core_off

    def block_copy(block, piece, send, peer):
        return remote(held.at[block, piece], held.at[block, piece], send, held_recv.at[block, piece], peer)

    def to_right(line, piece):
        return block_copy(at(line, 0, 0), piece, right_send.at[line, piece], (me + 4) % devices)

    def to_left(line, piece):
        return block_copy(at(line, 0, 0), piece, left_send.at[line, piece], (me + devices - 4) % devices)

    def to_chip(line, piece):
        return block_copy(at(line, 0, 0), piece, chip_send.at[line, piece], at(level, 1, 0))

    def to_core(line, chip_off, piece):
        return block_copy(at(line, chip_off, 0), piece, core_send.at[line, chip_off, piece], at(level, 0, 1))

    def arrived(line, chip_off, core_off, piece):
        block = at(line, chip_off, core_off)
        block_copy(block, piece, held_recv.at[block, piece], partner).wait_recv()

    def sides(d, action):
        pl.when(level >= d)(lambda: action(level - d, 1))
        pl.when(level + d <= last)(lambda: action(level + d, -1))

    def own(piece):
        pl.when(level < last)(lambda: to_right(level, piece).start())
        pl.when(level > 0)(lambda: to_left(level, piece).start())
        to_chip(level, piece).start()
        to_core(level, 0, piece).start()

    def line_step(d, piece):
        def take(line, sign):
            arrived(line, 0, 0, piece)
            if d < last:
                if sign > 0:
                    pl.when(level < last)(lambda: to_right(line, piece).start())
                else:
                    pl.when(level > 0)(lambda: to_left(line, piece).start())
            to_chip(line, piece).start()
            to_core(line, 0, piece).start()

        sides(d, take)

    def chip_step(d, piece):
        def take(line, sign):
            arrived(line, 1, 0, piece)
            to_core(line, 1, piece).start()

        if d == 0:
            take(level, 0)
        else:
            sides(d, take)

    def core_step(piece):
        for chip_off in range(2):
            for line in range(last + 1):
                arrived(line, chip_off, 1, piece)

    bins = NBIN // PIECES

    def turn(piece):
        for pair in range(WINDOWS // 2):
            block = held[:, piece, pair * 2 * channels : (pair + 1) * 2 * channels, :].astype(jnp.float32)
            for half in range(2):
                turned = block[:, half * channels : (half + 1) * channels].reshape(devices * channels, 2 * bins).T
                window = pair * 2 + half
                spectra_ref[piece % 2, pl.ds(window, bins, PITCH), :] = turned[:bins]
                spectra_ref[piece % 2, pl.ds(WINDOWS + window, bins, PITCH), :] = turned[bins:]

    def multiply(piece):
        span = 16 * WINDOWS
        place = lax.broadcasted_iota(jnp.int32, (HALF, span), 1) // (2 * WINDOWS)
        odd = lax.broadcasted_iota(jnp.int32, (span, TILE), 0) // (2 * WINDOWS) % 2
        upper = lax.broadcasted_iota(jnp.int32, (span, TILE), 1) < HALF

        def eight_bins(g):
            spans = [spectra_ref[piece % 2, pl.ds((g * 8 + k) * PITCH, 2 * WINDOWS), :] for k in range(8)]
            right = jnp.concatenate(spans, 0)
            split = right.reshape(8, 2, WINDOWS, TILE)
            turned = jnp.concatenate([split[:, 1:], -split[:, :1]], 1).reshape(span, TILE)
            both = jnp.concatenate([right, turned], 1).astype(jnp.bfloat16)
            narrow = jnp.where(upper, pltpu.roll(right, HALF, 1), turned)
            pairs = jnp.concatenate([jnp.where(odd == k, narrow, 0.0) for k in range(2)], 1).astype(jnp.bfloat16)
            left = right.T
            picked = [jnp.where(place == k, left[:HALF], 0.0).astype(jnp.bfloat16) for k in range(8)]
            wide = contract(jnp.concatenate(picked, 0), both, 1, 0)
            picked = [jnp.where(place // 2 == k, left[HALF:], 0.0).astype(jnp.bfloat16) for k in range(4)]
            paired = contract(jnp.concatenate(picked, 0), pairs, 1, 0)
            for k in range(8):
                f = piece * bins + g * 8 + k
                cross_ref[pl.ds(f, HALF, STRIDE), :] = wide[k * HALF : (k + 1) * HALF, :TILE]
                cross_ref[pl.ds(f + NBIN, HALF, STRIDE), :] = wide[k * HALF : (k + 1) * HALF, TILE:]
                column = k % 2 * TILE
                cross_ref[pl.ds(UPPER + f, HALF, NARROW), :] = paired[
                    k // 2 * HALF : (k // 2 + 1) * HALF, column : column + TILE
                ]

        for g in range(bins // 8):
            eight_bins(g)

    for piece in range(PIECES):
        own(piece)
    for d in range(1, last + 1):
        for piece in range(PIECES):
            line_step(d, piece)
        for piece in range(PIECES):
            chip_step(d - 1, piece)
    chip_step(last, 0)
    chip_step(last, 1)
    core_step(0)
    turn(0)
    chip_step(last, 2)
    chip_step(last, 3)
    core_step(1)
    turn(1)
    multiply(0)
    core_step(2)
    core_step(3)
    turn(2)
    multiply(1)
    turn(3)
    multiply(2)
    multiply(3)

    for piece in range(PIECES):
        pl.when(level < last)(lambda: to_right(level, piece).wait_send())
        pl.when(level > 0)(lambda: to_left(level, piece).wait_send())
        to_chip(level, piece).wait_send()
        to_core(level, 0, piece).wait_send()
        to_core(level, 1, piece).wait_send()
        for d in range(1, last + 1):
            def drain(line, sign):
                if d < last:
                    if sign > 0:
                        pl.when(level < last)(lambda: to_right(line, piece).wait_send())
                    else:
                        pl.when(level > 0)(lambda: to_left(line, piece).wait_send())
                to_chip(line, piece).wait_send()
                to_core(line, 0, piece).wait_send()
                to_core(line, 1, piece).wait_send()

            sides(d, drain)

    pair.wait_send()
    common_copy(core).wait_send()
    for k in range(1, chips):
        sum_copy(here, k).wait_send()


def tile_cross(devices, raw, fir, keep):
    rows = raw.shape[0] * raw.shape[1]
    dma = pltpu.SemaphoreType.DMA
    vmem = pl.BlockSpec(memory_space=pltpu.VMEM)
    hbm = pl.BlockSpec(memory_space=pltpu.HBM)
    half = (2, WINDOWS // 2, SEG)
    return pl.pallas_call(
        functools.partial(tile_kernel, devices),
        out_shape=pltpu.VMEM((UPPER + HALF * NARROW, TILE), jnp.float32),
        in_specs=[hbm] * 4,
        out_specs=vmem,
        scratch_shapes=[
            pltpu.VMEM(raw.shape, jnp.bfloat16), pltpu.VMEM((1, TAPS), jnp.float32),
            pltpu.VMEM(keep.shape[::-1], jnp.int32), pltpu.VMEM((2 * SEG, 2 * NBIN), jnp.bfloat16), dma((4,)),
            pltpu.VMEM(half, jnp.float32), pltpu.VMEM(half[1:], jnp.float32),
            pltpu.VMEM((devices // 2,) + half[1:], jnp.float32), pltpu.VMEM(half, jnp.float32),
            pltpu.VMEM((devices, PIECES, rows, 2 * NBIN // PIECES), jnp.bfloat16),
            pltpu.VMEM((2, PITCH * NBIN // PIECES, TILE), jnp.float32),
            dma, dma, dma((devices // 2,)), dma((devices // 2,)), dma, dma,
            dma((4, PIECES)), dma((4, PIECES)), dma((4, PIECES)), dma((4, 2, PIECES)), dma((devices, PIECES)),
        ],
        compiler_params=pltpu.CompilerParams(
            collective_id=0, has_side_effects=True, vmem_limit_bytes=10 << 20
        ),
    )(*[pltpu.with_memory_space_constraint(x, pltpu.HBM) for x in (raw, fir.reshape(1, TAPS), keep.T, piece_tables())])


def lag_kernel(per_step, cross_ref, lag_ref, out_ref, mirror_ref):
    base = pl.program_id(0) * per_step

    @pl.when(base < HALF)
    def _():
        for group in range(0, per_step, 4):
            turned = [
                cross_ref[pl.ds((base + group + k) * STRIDE, 2 * NBIN), :].astype(jnp.bfloat16).T for k in range(4)
            ]
            near = contract(jnp.concatenate([t[:HALF] for t in turned], 0), lag_ref[...], 1, 0)
            far = jnp.concatenate([t[HALF:] for t in turned], 0)
            even = contract(far[:, :NBIN], lag_ref[:NBIN, :], 1, 0)
            odd = contract(far[:, NBIN:], lag_ref[NBIN:, :], 1, 0)
            mirrored = even - odd
            out_ref[group : group + 4, :HALF] = near.reshape(4, HALF, LAGS).astype(jnp.bfloat16)
            out_ref[group : group + 4, HALF:] = (even + odd).reshape(4, HALF, LAGS).astype(jnp.bfloat16)
            for k in range(4):
                for part in range(LAGS // 128):
                    mirror_ref[part, pl.ds(base + group + k, HALF, TURN), :] = mirrored[
                        k * HALF : (k + 1) * HALF, part * 128 : (part + 1) * 128
                    ]

    @pl.when(base >= HALF)
    def _():
        for group in range(0, per_step, 4):
            rows = []
            for k in range(4):
                row = base - HALF + group + k
                turned = cross_ref[pl.ds(UPPER + row * NARROW, NBIN), :].astype(jnp.bfloat16).T
                rows.append(jnp.concatenate([turned[:HALF], turned[HALF:]], 1))
                parts = [mirror_ref[part, pl.ds(row * TURN, HALF), :] for part in range(LAGS // 128)]
                out_ref[group + k, :HALF] = jnp.concatenate(parts, 1).astype(jnp.bfloat16)
            far = contract(jnp.concatenate(rows, 0), lag_ref[...], 1, 0)
            out_ref[group : group + 4, HALF:] = far.reshape(4, HALF, LAGS).astype(jnp.bfloat16)


def tile_stack(cross):
    per_step = 32
    vmem = pl.BlockSpec(memory_space=pltpu.VMEM)
    return pl.pallas_call(
        functools.partial(lag_kernel, per_step),
        out_shape=jax.ShapeDtypeStruct((TILE, TILE, LAGS), jnp.bfloat16),
        grid=(TILE // per_step,),
        in_specs=[vmem, vmem],
        out_specs=pl.BlockSpec((per_step, TILE, LAGS), lambda s: (s, 0, 0)),
        scratch_shapes=[pltpu.VMEM((LAGS // 128, HALF * TURN, 128), jnp.float32)],
        compiler_params=pltpu.CompilerParams(vmem_limit_bytes=16 << 20),
        cost_estimate=pl.CostEstimate(flops=5 << 30, bytes_accessed=12 << 20, transcendentals=0),
    )(cross, lag_table())


def local(raw, fir, keep, table):
    devices = lax.axis_size("tiles")
    if devices == WINDOWS and devices * raw.shape[1] == TILE:
        return tile_stack(tile_cross(devices, raw, fir, keep))[None]
    gathered = front(devices, raw, fir, keep)
    return stack(gathered, table)[None]


def solution(mesh):
    placed = (P(None, ("groups", "tiles"), None), P(), P(None, ("groups", "tiles")), P())
    return jax.shard_map(
        local,
        mesh=mesh,
        in_specs=placed,
        out_specs=P(("groups", "tiles"), None, None, None),
        check_vma=False,
    )
```

```python
import functools

import jax
import jax.numpy as jnp
import numpy as np
from jax import lax
from jax.experimental import pallas as pl
from jax.experimental.pallas import tpu as pltpu
from jax.sharding import PartitionSpec as P

WINDOWS = 16
TILE = 128
SEG = 512
LAGS = 256
TAPS = 64
DEC = 4
RAW = 2048
NBIN = 256
SPAN = 640
STRIDE = 521
PIECES = 4


def split2(x):
    high = x.astype(jnp.bfloat16)
    return high, (x - high.astype(jnp.float32)).astype(jnp.bfloat16)


def split3(x):
    high = x.astype(jnp.bfloat16)
    rest = x - high.astype(jnp.float32)
    middle = rest.astype(jnp.bfloat16)
    return high, middle, (rest - middle.astype(jnp.float32)).astype(jnp.bfloat16)


def contract(a, b, left, right):
    return lax.dot_general(a, b, (((left,), (right,)), ((), ())), preferred_element_type=jnp.float32)


def dft_tables():
    angle = 2.0 * np.pi / SEG * np.mod(np.arange(SEG)[:, None] * np.arange(NBIN)[None, :], SEG)
    table = np.concatenate([np.cos(angle), -np.sin(angle)], 1).astype(np.float32)
    high = table.astype(jnp.bfloat16)
    low = (table - high.astype(np.float32)).astype(jnp.bfloat16)
    return jnp.asarray(np.concatenate([high, low], 0))


def lag_table():
    freqs = np.arange(NBIN)
    shifts = np.arange(LAGS) - LAGS // 2
    angle = 2.0 * np.pi / SEG * np.mod(freqs[:, None] * shifts[None, :], SEG)
    weight = np.where(freqs == 0, 1.0, 2.0)[:, None] / np.sqrt(WINDOWS * NBIN)
    table = np.concatenate([weight * np.cos(angle), -weight * np.sin(angle)], 0)
    return jnp.asarray(table.astype(np.float32).astype(jnp.bfloat16))


def filter_rows(raw_ref, taps_ref):
    rows = raw_ref.shape[0] * raw_ref.shape[1]
    raw = raw_ref[...].astype(jnp.float32).reshape(rows, RAW).astype(jnp.bfloat16)
    taps = jnp.broadcast_to(taps_ref[...], (8, TAPS))
    places = lax.broadcasted_iota(jnp.int32, (TAPS, SPAN), 0) + lax.broadcasted_iota(jnp.int32, (TAPS, SPAN), 1)
    pick = jnp.where(places == TILE, 1.0, 0.0).astype(jnp.bfloat16)
    spread = sum(contract(part, pick, 1, 0) for part in split3(taps)[::-1])
    band = jnp.broadcast_to(spread[:1], (TILE, SPAN))
    index = lax.broadcasted_iota(jnp.int32, (TILE, SPAN), 0)
    for bit in range(7):
        band = jnp.where((index >> bit) & 1 == 1, pltpu.roll(band, DEC << bit, 1), band)
    pieces = [jnp.concatenate([jnp.zeros((rows, TILE), jnp.bfloat16), raw[:, :SEG]], 1)]
    for block in range(1, RAW // SEG):
        pieces.append(raw[:, block * SEG - TILE : (block + 1) * SEG])
    spans = jnp.concatenate(pieces, 0)
    out = sum(contract(spans, part, 1, 1) for part in split3(band)[::-1])
    return jnp.concatenate([out[b * rows : (b + 1) * rows] for b in range(RAW // SEG)], 1)


def whiten_rows(decimated, keep, table_ref):
    high, low = split2(decimated)
    table_high = table_ref[:SEG, :]
    spectrum = contract(low, table_high, 1, 0) + contract(high, table_ref[SEG:, :], 1, 0)
    spectrum = spectrum + contract(high, table_high, 1, 0)
    real_part, imag_part = spectrum[:, :NBIN], spectrum[:, NBIN:]
    power = real_part * real_part + imag_part * imag_part
    level = jnp.mean(power, -1, keepdims=True)
    scale = keep.astype(jnp.float32) * lax.rsqrt(0.5 * power + 0.5 * level + 1e-05)
    return jnp.concatenate([real_part * scale, imag_part * scale], 1).astype(jnp.bfloat16)


def arrange(piece_ref, spectra_ref):
    members, rows = piece_ref.shape[:2]
    width = rows // WINDOWS
    for pair in range(WINDOWS // 2):
        for quarter in range(4):
            block = piece_ref[:, pair * 2 * width : (pair + 1) * 2 * width, quarter * 128 : (quarter + 1) * 128]
            block = block.astype(jnp.float32)
            for half in range(2):
                turned = block[:, half * width : (half + 1) * width].reshape(members * width, 128).T
                start = (quarter % 2) * 128 * 32 + (quarter // 2) * WINDOWS + pair * 2 + half
                spectra_ref[pl.ds(start, 128, 32), :] = turned


def stack_kernel(same, per_step, *refs):
    if same:
        rows_ref, lag_ref, out_ref, cross_ref, row_spec = refs
    else:
        _, rows_ref, cols_ref, lag_ref, out_ref, cross_ref, row_spec, col_spec = refs

    @pl.when(pl.program_id(0) == 0)
    def _():
        arrange(rows_ref, row_spec)
        if not same:
            arrange(cols_ref, col_spec)

        def one_bin(f, carry):
            start = pl.multiple_of(f * 32, 32)
            left = row_spec[pl.ds(start, 32), :]
            right = left if same else col_spec[pl.ds(start, 32), :]
            turned = jnp.concatenate([right[WINDOWS:], -right[:WINDOWS]], 0)
            both = jnp.concatenate([right, turned], 1).astype(jnp.bfloat16)
            cross = contract(left.astype(jnp.bfloat16), both, 0, 0)
            cross_ref[pl.ds(f, TILE, STRIDE), :] = cross[:, :TILE]
            cross_ref[pl.ds(f + NBIN, TILE, STRIDE), :] = cross[:, TILE:]
            return carry

        lax.fori_loop(0, NBIN, one_bin, 0, unroll=64)

    base = pl.program_id(0) * per_step
    for group in range(per_step // 4):
        picked = []
        for member in range(4):
            start = (base + group * 4 + member) * STRIDE
            picked.append(cross_ref[pl.ds(start, 2 * NBIN), :].astype(jnp.bfloat16))
        stacked = contract(jnp.concatenate(picked, 1), lag_ref[...], 0, 0)
        out_ref[group * 4 : group * 4 + 4] = stacked.reshape(4, TILE, LAGS).astype(jnp.bfloat16)


def stack(gathered, table):
    members = TILE * WINDOWS // gathered.shape[1]
    same = gathered.shape[0] == members
    per_step = 32
    block = (members,) + gathered.shape[1:]
    spectra = pltpu.VMEM((2 * NBIN * WINDOWS, TILE), jnp.float32)
    if same:
        prefetch = []
        sides = [pl.BlockSpec(block, lambda s: (0, 0, 0))]
    else:
        prefetch = [table[lax.axis_index("tiles")]]
        sides = [
            pl.BlockSpec(block, lambda s, entry: (entry[0], 0, 0)),
            pl.BlockSpec(block, lambda s, entry: (entry[1], 0, 0)),
        ]
    return pl.pallas_call(
        functools.partial(stack_kernel, same, per_step),
        out_shape=jax.ShapeDtypeStruct((TILE, TILE, LAGS), jnp.bfloat16),
        grid_spec=pltpu.PrefetchScalarGridSpec(
            num_scalar_prefetch=len(prefetch),
            grid=(TILE // per_step,),
            in_specs=sides + [pl.BlockSpec((2 * NBIN, LAGS), lambda s, *entry: (0, 0))],
            out_specs=pl.BlockSpec((per_step, TILE, LAGS), lambda s, *entry: (s, 0, 0)),
            scratch_shapes=[pltpu.VMEM((TILE * STRIDE, TILE), jnp.float32)] + [spectra] * len(sides),
        ),
        compiler_params=pltpu.CompilerParams(vmem_limit_bytes=60 << 20),
        cost_estimate=pl.CostEstimate(flops=10 << 30, bytes_accessed=12 << 20, transcendentals=0),
    )(*prefetch, *[gathered] * len(sides), lag_table())


def other_core(me):
    return me + 1 - 2 * (me % 2)


def other_chip(me):
    return me + 2 - 4 * ((me // 2) % 2)


def remote(source, target, send, receive, peer):
    return pltpu.make_async_remote_copy(
        src_ref=source,
        dst_ref=target,
        send_sem=send,
        recv_sem=receive,
        device_id={"tiles": peer},
        device_id_type=pl.DeviceIdType.MESH,
    )


def front_kernel(
    devices, raw_hbm, taps_ref, keep_ref, table_hbm, out_ref,
    raw_ref, table_ref, load_sem, sum_buf, part_buf, common_buf, held,
    part_send, part_recv, common_send, common_recv,
    right_send, left_send, chip_send, core_send, held_recv, local_sem,
):
    me = lax.axis_index("tiles")
    channels = raw_ref.shape[1]
    rows = WINDOWS * channels
    barrier = pltpu.get_barrier_semaphore()
    all_owners = devices == WINDOWS

    def greet(k, carry):
        pl.semaphore_signal(
            barrier, inc=1, device_id={"tiles": (me + k) % devices}, device_id_type=pl.DeviceIdType.MESH
        )
        return carry

    lax.fori_loop(1, devices, greet, 0)
    load_raw = pltpu.make_async_copy(raw_hbm, raw_ref, load_sem.at[0])
    load_raw.start()
    load_table = pltpu.make_async_copy(table_hbm, table_ref, load_sem.at[1])
    load_table.start()
    load_raw.wait()
    filtered = filter_rows(raw_ref, taps_ref).reshape(WINDOWS, channels, SEG)
    sum_buf[...] = jnp.sum(filtered, 1, keepdims=True)
    pl.semaphore_wait(barrier, devices - 1)

    def part_copy(owner, slot):
        return remote(sum_buf.at[owner], part_buf.at[slot], part_send.at[owner], part_recv.at[slot], owner)

    def common_copy(owner, peer):
        return remote(common_buf.at[owner], common_buf.at[owner], common_send.at[peer], common_recv.at[owner], peer)

    def send_part(k, carry):
        owner = (me + k) % WINDOWS

        @pl.when(owner != me)
        def _():
            part_copy(owner, me).start()

        return carry

    lax.fori_loop(1 if all_owners else 0, WINDOWS, send_part, 0)

    @pl.when(me < WINDOWS)
    def _():
        part_buf[me] = sum_buf[me]

        def take(k, carry):
            part_copy(me, (me + k) % devices).wait_recv()
            return carry

        lax.fori_loop(1, devices, take, 0)
        common_buf[me] = jnp.sum(part_buf[...], 0)

        def give(k, carry):
            common_copy(me, (me + k) % devices).start()
            return carry

        lax.fori_loop(1, devices, give, 0)

    def take_common(k, carry):
        owner = (me + k) % WINDOWS

        @pl.when(owner != me)
        def _():
            common_copy(owner, me).wait_recv()

        return carry

    lax.fori_loop(1 if all_owners else 0, WINDOWS, take_common, 0)
    common = common_buf[...] / (channels * devices)
    decimated = (filtered - common).reshape(rows, SEG)
    keep = jnp.broadcast_to(keep_ref[...].astype(jnp.float32).T[:, :, None], (WINDOWS, channels, NBIN))
    load_table.wait()
    whitened = whiten_rows(decimated, keep.reshape(rows, NBIN), table_ref)
    held[me] = whitened.reshape(PIECES, rows // PIECES, 2 * NBIN)

    depth = devices // 4
    q, low = me // 4, me % 4
    chip, core = other_chip(me), other_core(me)

    def block_copy(block, piece, send, peer):
        return remote(held.at[block, piece], held.at[block, piece], send, held_recv.at[block, piece], peer)

    def to_right(level, piece):
        return block_copy(4 * level + low, piece, right_send.at[level, piece], (me + 4) % devices)

    def to_left(level, piece):
        return block_copy(4 * level + low, piece, left_send.at[level, piece], (me + devices - 4) % devices)

    def to_chip(level, piece):
        return block_copy(4 * level + low, piece, chip_send.at[level, piece], chip)

    def to_core(block, piece):
        return block_copy(block, piece, core_send.at[block // 2, piece], core)

    def local_copy(block, piece):
        part = rows // PIECES
        return pltpu.make_async_copy(
            held.at[block, piece], out_ref.at[block, pl.ds(piece * part, part)], local_sem.at[block, piece]
        )

    def arrived(block, piece):
        to_core(block, piece).wait_recv()
        local_copy(block, piece).start()

    def line_block(level, piece, forward, go):
        block = 4 * level + low
        arrived(block, piece)

        @pl.when(go)
        def _():
            forward(level, piece).start()

        to_chip(level, piece).start()
        to_core(block, piece).start()

    def chip_block(level, piece):
        block = 4 * level + other_chip(low)
        arrived(block, piece)
        to_core(block, piece).start()

    for piece in range(PIECES):
        @pl.when(q < depth - 1)
        def _():
            to_right(q, piece).start()

        @pl.when(q > 0)
        def _():
            to_left(q, piece).start()

        to_chip(q, piece).start()

    for piece in range(PIECES):
        to_core(me, piece).start()
        local_copy(me, piece).start()

    def step(d, carry):
        for piece in range(PIECES):
            @pl.when(q - d >= 0)
            def _():
                line_block(q - d, piece, to_right, q < depth - 1)

            @pl.when(q + d < depth)
            def _():
                line_block(q + d, piece, to_left, q > 0)

        for piece in range(PIECES):
            @pl.when(d == 1)
            def _():
                chip_block(q, piece)

            @pl.when((d > 1) & (q - d + 1 >= 0))
            def _():
                chip_block(q - d + 1, piece)

            @pl.when((d > 1) & (q + d - 1 < depth))
            def _():
                chip_block(q + d - 1, piece)

        return carry

    lax.fori_loop(1, depth + 1, step, 0)

    def from_core(pair, carry):
        for piece in range(PIECES):
            arrived(2 * pair + core % 2, piece)
        return carry

    lax.fori_loop(0, 2 * depth, from_core, 0)

    def finish(level, carry):
        for piece in range(PIECES):
            @pl.when((level <= q) & (q < depth - 1))
            def _():
                to_right(level, piece).wait_send()

            @pl.when((level >= q) & (q > 0))
            def _():
                to_left(level, piece).wait_send()

            to_chip(level, piece).wait_send()
            to_core(4 * level + low, piece).wait_send()
            to_core(4 * level + other_chip(low), piece).wait_send()
        return carry

    lax.fori_loop(0, depth, finish, 0)

    def drain_part(k, carry):
        owner = (me + k) % WINDOWS

        @pl.when(owner != me)
        def _():
            part_copy(owner, me).wait_send()

        return carry

    lax.fori_loop(1 if all_owners else 0, WINDOWS, drain_part, 0)

    @pl.when(me < WINDOWS)
    def _():
        def drain(k, carry):
            common_copy(me, (me + k) % devices).wait_send()
            return carry

        lax.fori_loop(1, devices, drain, 0)

    def settle(block, carry):
        for piece in range(PIECES):
            local_copy(block, piece).wait()
        return carry

    lax.fori_loop(0, devices, settle, 0)


def front(devices, raw, fir, keep):
    rows = raw.shape[0] * raw.shape[1]
    depth = devices // 4
    dma = pltpu.SemaphoreType.DMA
    vmem = pl.BlockSpec(memory_space=pltpu.VMEM)
    hbm = pl.BlockSpec(memory_space=pl.ANY)
    line = pltpu.VMEM((WINDOWS, 1, SEG), jnp.float32)
    return pl.pallas_call(
        functools.partial(front_kernel, devices),
        out_shape=jax.ShapeDtypeStruct((devices, rows, 2 * NBIN), jnp.bfloat16),
        in_specs=[hbm, vmem, vmem, hbm],
        out_specs=pl.BlockSpec(memory_space=pl.ANY),
        scratch_shapes=[
            pltpu.VMEM(raw.shape, jnp.bfloat16), pltpu.VMEM((2 * SEG, 2 * NBIN), jnp.bfloat16), dma((2,)),
            line, pltpu.VMEM((devices, 1, SEG), jnp.float32), line,
            pltpu.VMEM((devices, PIECES, rows // PIECES, 2 * NBIN), jnp.bfloat16),
            dma((WINDOWS,)), dma((devices,)), dma((devices,)), dma((WINDOWS,)),
            dma((depth, PIECES)), dma((depth, PIECES)), dma((depth, PIECES)), dma((2 * depth, PIECES)),
            dma((devices, PIECES)), dma((devices, PIECES)),
        ],
        compiler_params=pltpu.CompilerParams(
            collective_id=0, has_side_effects=True, vmem_limit_bytes=60 << 20
        ),
    )(raw, fir.reshape(1, TAPS), keep.T, dft_tables())


def piece_tables():
    angle = 2.0 * np.pi / SEG * np.mod(np.arange(SEG)[:, None] * np.arange(NBIN)[None, :], SEG)
    bins = NBIN // PIECES
    cosine, sine = np.cos(angle).reshape(SEG, PIECES, bins), -np.sin(angle).reshape(SEG, PIECES, bins)
    table = np.concatenate([cosine, sine], 2).reshape(SEG, 2 * NBIN).astype(np.float32)
    high = table.astype(jnp.bfloat16)
    low = (table - high.astype(np.float32)).astype(jnp.bfloat16)
    return jnp.asarray(np.concatenate([high, low], 0))


def whiten_pieces(decimated, keep, table_ref):
    high, low = split2(decimated)
    table_high = table_ref[:SEG, :]
    spectrum = contract(low, table_high, 1, 0) + contract(high, table_ref[SEG:, :], 1, 0)
    spectrum = spectrum + contract(high, table_high, 1, 0)
    width = 2 * NBIN // PIECES
    parts = [spectrum[:, p * width : (p + 1) * width] for p in range(PIECES)]
    squares = [part * part for part in parts]
    level = jnp.sum(sum(squares), -1, keepdims=True) / NBIN
    whitened = []
    for part, square in zip(parts, squares):
        power = square + pltpu.roll(square, width // 2, 1)
        scale = keep * lax.rsqrt(0.5 * power + 0.5 * level + 1e-05)
        whitened.append((part * scale).astype(jnp.bfloat16))
    return whitened


PITCH = 33
HALF = TILE // 2
UPPER = HALF * STRIDE
NARROW = NBIN + 1
TURN = HALF + 1


def tile_kernel(
    devices, raw_hbm, taps_hbm, keep_hbm, table_hbm, cross_ref,
    raw_ref, taps_ref, keep_ref, table_ref, load_sem,
    sum_buf, pair_buf, chip_buf, common_buf, held, spectra_ref,
    pair_send, pair_recv, sum_send, sum_recv, common_send, common_recv,
    right_send, left_send, chip_send, core_send, held_recv,
):
    me = lax.axis_index("tiles")
    channels = raw_ref.shape[1]
    rows = WINDOWS * channels
    chips = devices // 2
    here, core = me // 2, me % 2
    partner = 2 * here + 1 - core
    barrier = pltpu.get_barrier_semaphore()

    def greet(device):
        pl.semaphore_signal(
            barrier, inc=1, device_id={"tiles": device}, device_id_type=pl.DeviceIdType.MESH
        )

    greet(partner)
    for k in range(1, chips):
        greet(2 * ((here + k) % chips) + core)
    load_raw = pltpu.make_async_copy(raw_hbm, raw_ref, load_sem.at[0])
    load_raw.start()
    load_taps = pltpu.make_async_copy(taps_hbm, taps_ref, load_sem.at[2])
    load_taps.start()
    load_keep = pltpu.make_async_copy(keep_hbm, keep_ref, load_sem.at[3])
    load_keep.start()
    load_table = pltpu.make_async_copy(table_hbm, table_ref, load_sem.at[1])
    load_table.start()
    load_taps.wait()
    load_raw.wait()
    filtered = filter_rows(raw_ref, taps_ref).reshape(WINDOWS, channels, SEG)
    sum_buf[...] = jnp.sum(filtered, 1).reshape(sum_buf.shape)
    pl.semaphore_wait(barrier, chips)

    pair = remote(sum_buf.at[1 - core], pair_buf, pair_send, pair_recv, partner)
    pair.start()
    pair.wait_recv()
    chip_buf[here] = sum_buf[core] + pair_buf[...]

    def sum_copy(chip, k):
        return remote(
            chip_buf.at[chip], chip_buf.at[chip], sum_send.at[k], sum_recv.at[chip], 2 * ((here + k) % chips) + core
        )

    for k in range(1, chips):
        sum_copy(here, k).start()
    for k in range(1, chips):
        sum_copy((here + k) % chips, k).wait_recv()
    common_buf[core] = jnp.sum(chip_buf[...], 0)

    def common_copy(half):
        return remote(common_buf.at[half], common_buf.at[half], common_send, common_recv, partner)

    common_copy(core).start()
    common_copy(1 - core).wait_recv()
    common = common_buf[...].reshape(WINDOWS, 1, SEG) / (channels * devices)
    decimated = (filtered - common).reshape(rows, SEG)
    load_keep.wait()
    keep = jnp.broadcast_to(keep_ref[...].astype(jnp.float32).T[:, :, None], (WINDOWS, channels, 128))
    load_table.wait()
    whitened = whiten_pieces(decimated, keep.reshape(rows, 128), table_ref)

    level, chip = me // 4, (me // 2) % 2
    last = devices // 4 - 1

    def at(line, chip_off, core_off):
        return 4 * line + 2 * (chip + chip_off - 2 * chip * chip_off) + core + core_off - 2 * core * core_off

    def block_copy(block, piece, send, peer):
        return remote(held.at[block, piece], held.at[block, piece], send, held_recv.at[block, piece], peer)

    def to_right(line, piece):
        return block_copy(at(line, 0, 0), piece, right_send.at[line, piece], (me + 4) % devices)

    def to_left(line, piece):
        return block_copy(at(line, 0, 0), piece, left_send.at[line, piece], (me + devices - 4) % devices)

    def to_chip(line, piece):
        return block_copy(at(line, 0, 0), piece, chip_send.at[line, piece], at(level, 1, 0))

    def to_core(line, chip_off, piece):
        return block_copy(at(line, chip_off, 0), piece, core_send.at[line, chip_off, piece], at(level, 0, 1))

    def arrived(line, chip_off, core_off, piece):
        block = at(line, chip_off, core_off)
        block_copy(block, piece, held_recv.at[block, piece], partner).wait_recv()

    def sides(d, action):
        pl.when(level >= d)(lambda: action(level - d, 1))
        pl.when(level + d <= last)(lambda: action(level + d, -1))

    def own(piece):
        pl.when(level < last)(lambda: to_right(level, piece).start())
        pl.when(level > 0)(lambda: to_left(level, piece).start())
        to_chip(level, piece).start()
        to_core(level, 0, piece).start()

    def line_step(d, piece):
        def take(line, sign):
            arrived(line, 0, 0, piece)
            if d < last:
                if sign > 0:
                    pl.when(level < last)(lambda: to_right(line, piece).start())
                else:
                    pl.when(level > 0)(lambda: to_left(line, piece).start())
            to_chip(line, piece).start()
            to_core(line, 0, piece).start()

        sides(d, take)

    def chip_step(d, piece):
        def take(line, sign):
            arrived(line, 1, 0, piece)
            to_core(line, 1, piece).start()

        if d == 0:
            take(level, 0)
        else:
            sides(d, take)

    def core_step(piece):
        for chip_off in range(2):
            for line in range(last + 1):
                arrived(line, chip_off, 1, piece)

    bins = NBIN // PIECES

    def turn(piece):
        for pair in range(WINDOWS // 2):
            block = held[:, piece, pair * 2 * channels : (pair + 1) * 2 * channels, :].astype(jnp.float32)
            for half in range(2):
                turned = block[:, half * channels : (half + 1) * channels].reshape(devices * channels, 2 * bins).T
                window = pair * 2 + half
                spectra_ref[piece % 2, pl.ds(window, bins, PITCH), :] = turned[:bins]
                spectra_ref[piece % 2, pl.ds(WINDOWS + window, bins, PITCH), :] = turned[bins:]

    def multiply(piece):
        span = 16 * WINDOWS
        place = lax.broadcasted_iota(jnp.int32, (HALF, span), 1) // (2 * WINDOWS)
        odd = lax.broadcasted_iota(jnp.int32, (span, TILE), 0) // (2 * WINDOWS) % 2
        upper = lax.broadcasted_iota(jnp.int32, (span, TILE), 1) < HALF

        def eight_bins(g):
            spans = [spectra_ref[piece % 2, pl.ds((g * 8 + k) * PITCH, 2 * WINDOWS), :] for k in range(8)]
            right = jnp.concatenate(spans, 0)
            split = right.reshape(8, 2, WINDOWS, TILE)
            turned = jnp.concatenate([split[:, 1:], -split[:, :1]], 1).reshape(span, TILE)
            both = jnp.concatenate([right, turned], 1).astype(jnp.bfloat16)
            narrow = jnp.where(upper, pltpu.roll(right, HALF, 1), turned)
            pairs = jnp.concatenate([jnp.where(odd == k, narrow, 0.0) for k in range(2)], 1).astype(jnp.bfloat16)
            left = right.T
            picked = [jnp.where(place == k, left[:HALF], 0.0).astype(jnp.bfloat16) for k in range(8)]
            wide = contract(jnp.concatenate(picked, 0), both, 1, 0)
            picked = [jnp.where(place // 2 == k, left[HALF:], 0.0).astype(jnp.bfloat16) for k in range(4)]
            paired = contract(jnp.concatenate(picked, 0), pairs, 1, 0)
            for k in range(8):
                f = piece * bins + g * 8 + k
                cross_ref[pl.ds(f, HALF, STRIDE), :] = wide[k * HALF : (k + 1) * HALF, :TILE]
                cross_ref[pl.ds(f + NBIN, HALF, STRIDE), :] = wide[k * HALF : (k + 1) * HALF, TILE:]
                column = k % 2 * TILE
                cross_ref[pl.ds(UPPER + f, HALF, NARROW), :] = paired[
                    k // 2 * HALF : (k // 2 + 1) * HALF, column : column + TILE
                ]

        for g in range(bins // 8):
            eight_bins(g)

    for piece in range(PIECES):
        held[me, piece] = whitened[piece]
        own(piece)
    for d in range(1, last + 1):
        for piece in range(PIECES):
            line_step(d, piece)
        for piece in range(PIECES):
            chip_step(d - 1, piece)
    chip_step(last, 0)
    chip_step(last, 1)
    core_step(0)
    turn(0)
    chip_step(last, 2)
    chip_step(last, 3)
    core_step(1)
    turn(1)
    multiply(0)
    core_step(2)
    core_step(3)
    turn(2)
    multiply(1)
    turn(3)
    multiply(2)
    multiply(3)

    for piece in range(PIECES):
        pl.when(level < last)(lambda: to_right(level, piece).wait_send())
        pl.when(level > 0)(lambda: to_left(level, piece).wait_send())
        to_chip(level, piece).wait_send()
        to_core(level, 0, piece).wait_send()
        to_core(level, 1, piece).wait_send()
        for d in range(1, last + 1):
            def drain(line, sign):
                if d < last:
                    if sign > 0:
                        pl.when(level < last)(lambda: to_right(line, piece).wait_send())
                    else:
                        pl.when(level > 0)(lambda: to_left(line, piece).wait_send())
                to_chip(line, piece).wait_send()
                to_core(line, 0, piece).wait_send()
                to_core(line, 1, piece).wait_send()

            sides(d, drain)

    pair.wait_send()
    common_copy(core).wait_send()
    for k in range(1, chips):
        sum_copy(here, k).wait_send()


def tile_cross(devices, raw, fir, keep):
    rows = raw.shape[0] * raw.shape[1]
    dma = pltpu.SemaphoreType.DMA
    vmem = pl.BlockSpec(memory_space=pltpu.VMEM)
    hbm = pl.BlockSpec(memory_space=pltpu.HBM)
    half = (2, WINDOWS // 2, SEG)
    return pl.pallas_call(
        functools.partial(tile_kernel, devices),
        out_shape=pltpu.VMEM((UPPER + HALF * NARROW, TILE), jnp.float32),
        in_specs=[hbm] * 4,
        out_specs=vmem,
        scratch_shapes=[
            pltpu.VMEM(raw.shape, jnp.bfloat16), pltpu.VMEM((1, TAPS), jnp.float32),
            pltpu.VMEM(keep.shape[::-1], jnp.int32), pltpu.VMEM((2 * SEG, 2 * NBIN), jnp.bfloat16), dma((4,)),
            pltpu.VMEM(half, jnp.float32), pltpu.VMEM(half[1:], jnp.float32),
            pltpu.VMEM((devices // 2,) + half[1:], jnp.float32), pltpu.VMEM(half, jnp.float32),
            pltpu.VMEM((devices, PIECES, rows, 2 * NBIN // PIECES), jnp.bfloat16),
            pltpu.VMEM((2, PITCH * NBIN // PIECES, TILE), jnp.float32),
            dma, dma, dma((devices // 2,)), dma((devices // 2,)), dma, dma,
            dma((4, PIECES)), dma((4, PIECES)), dma((4, PIECES)), dma((4, 2, PIECES)), dma((devices, PIECES)),
        ],
        compiler_params=pltpu.CompilerParams(
            collective_id=0, has_side_effects=True, vmem_limit_bytes=10 << 20
        ),
    )(*[pltpu.with_memory_space_constraint(x, pltpu.HBM) for x in (raw, fir.reshape(1, TAPS), keep.T, piece_tables())])


def lag_kernel(per_step, cross_ref, lag_ref, out_ref, mirror_ref):
    base = pl.program_id(0) * per_step

    @pl.when(base < HALF)
    def _():
        for group in range(0, per_step, 4):
            turned = [
                cross_ref[pl.ds((base + group + k) * STRIDE, 2 * NBIN), :].astype(jnp.bfloat16).T for k in range(4)
            ]
            near = contract(jnp.concatenate([t[:HALF] for t in turned], 0), lag_ref[...], 1, 0)
            far = jnp.concatenate([t[HALF:] for t in turned], 0)
            even = contract(far[:, :NBIN], lag_ref[:NBIN, :], 1, 0)
            odd = contract(far[:, NBIN:], lag_ref[NBIN:, :], 1, 0)
            mirrored = even - odd
            out_ref[group : group + 4, :HALF] = near.reshape(4, HALF, LAGS).astype(jnp.bfloat16)
            out_ref[group : group + 4, HALF:] = (even + odd).reshape(4, HALF, LAGS).astype(jnp.bfloat16)
            for k in range(4):
                for part in range(LAGS // 128):
                    mirror_ref[part, pl.ds(base + group + k, HALF, TURN), :] = mirrored[
                        k * HALF : (k + 1) * HALF, part * 128 : (part + 1) * 128
                    ]

    @pl.when(base >= HALF)
    def _():
        for group in range(0, per_step, 4):
            rows = []
            for k in range(4):
                row = base - HALF + group + k
                turned = cross_ref[pl.ds(UPPER + row * NARROW, NBIN), :].astype(jnp.bfloat16).T
                rows.append(jnp.concatenate([turned[:HALF], turned[HALF:]], 1))
                parts = [mirror_ref[part, pl.ds(row * TURN, HALF), :] for part in range(LAGS // 128)]
                out_ref[group + k, :HALF] = jnp.concatenate(parts, 1).astype(jnp.bfloat16)
            far = contract(jnp.concatenate(rows, 0), lag_ref[...], 1, 0)
            out_ref[group : group + 4, HALF:] = far.reshape(4, HALF, LAGS).astype(jnp.bfloat16)


def tile_stack(cross):
    per_step = 64
    vmem = pl.BlockSpec(memory_space=pltpu.VMEM)
    return pl.pallas_call(
        functools.partial(lag_kernel, per_step),
        out_shape=jax.ShapeDtypeStruct((TILE, TILE, LAGS), jnp.bfloat16),
        grid=(TILE // per_step,),
        in_specs=[vmem, vmem],
        out_specs=pl.BlockSpec((per_step, TILE, LAGS), lambda s: (s, 0, 0)),
        scratch_shapes=[pltpu.VMEM((LAGS // 128, HALF * TURN, 128), jnp.float32)],
        compiler_params=pltpu.CompilerParams(vmem_limit_bytes=22 << 20),
        cost_estimate=pl.CostEstimate(flops=5 << 30, bytes_accessed=12 << 20, transcendentals=0),
    )(cross, lag_table())


def local(raw, fir, keep, table):
    devices = lax.axis_size("tiles")
    if devices == WINDOWS and devices * raw.shape[1] == TILE:
        return tile_stack(tile_cross(devices, raw, fir, keep))[None]
    gathered = front(devices, raw, fir, keep)
    return stack(gathered, table)[None]


def solution(mesh):
    placed = (P(None, ("groups", "tiles"), None), P(), P(None, ("groups", "tiles")), P())
    return jax.shard_map(
        local,
        mesh=mesh,
        in_specs=placed,
        out_specs=P(("groups", "tiles"), None, None, None),
        check_vma=False,
    )
```

```python
import functools

import jax
import jax.numpy as jnp
import numpy as np
from jax import lax
from jax.experimental import pallas as pl
from jax.experimental.pallas import tpu as pltpu
from jax.sharding import PartitionSpec as P

WINDOWS = 16
TILE = 128
SEG = 512
LAGS = 256
TAPS = 64
DEC = 4
RAW = 2048
NBIN = 256
SPAN = 640
STRIDE = 521
PIECES = 4


def split2(x):
    high = x.astype(jnp.bfloat16)
    return high, (x - high.astype(jnp.float32)).astype(jnp.bfloat16)


def split3(x):
    high = x.astype(jnp.bfloat16)
    rest = x - high.astype(jnp.float32)
    middle = rest.astype(jnp.bfloat16)
    return high, middle, (rest - middle.astype(jnp.float32)).astype(jnp.bfloat16)


def contract(a, b, left, right):
    return lax.dot_general(a, b, (((left,), (right,)), ((), ())), preferred_element_type=jnp.float32)


def dft_tables():
    angle = 2.0 * np.pi / SEG * np.mod(np.arange(SEG)[:, None] * np.arange(NBIN)[None, :], SEG)
    table = np.concatenate([np.cos(angle), -np.sin(angle)], 1).astype(np.float32)
    high = table.astype(jnp.bfloat16)
    low = (table - high.astype(np.float32)).astype(jnp.bfloat16)
    return jnp.asarray(np.concatenate([high, low], 0))


def lag_table():
    freqs = np.arange(NBIN)
    shifts = np.arange(LAGS) - LAGS // 2
    angle = 2.0 * np.pi / SEG * np.mod(freqs[:, None] * shifts[None, :], SEG)
    weight = np.where(freqs == 0, 1.0, 2.0)[:, None] / np.sqrt(WINDOWS * NBIN)
    table = np.concatenate([weight * np.cos(angle), -weight * np.sin(angle)], 0)
    return jnp.asarray(table.astype(np.float32).astype(jnp.bfloat16))


def filter_rows(raw_ref, taps_ref):
    rows = raw_ref.shape[0] * raw_ref.shape[1]
    raw = raw_ref[...].astype(jnp.float32).reshape(rows, RAW).astype(jnp.bfloat16)
    taps = jnp.broadcast_to(taps_ref[...], (8, TAPS))
    places = lax.broadcasted_iota(jnp.int32, (TAPS, SPAN), 0) + lax.broadcasted_iota(jnp.int32, (TAPS, SPAN), 1)
    pick = jnp.where(places == TILE, 1.0, 0.0).astype(jnp.bfloat16)
    spread = sum(contract(part, pick, 1, 0) for part in split3(taps)[::-1])
    band = jnp.broadcast_to(spread[:1], (TILE, SPAN))
    index = lax.broadcasted_iota(jnp.int32, (TILE, SPAN), 0)
    for bit in range(7):
        band = jnp.where((index >> bit) & 1 == 1, pltpu.roll(band, DEC << bit, 1), band)
    pieces = [jnp.concatenate([jnp.zeros((rows, TILE), jnp.bfloat16), raw[:, :SEG]], 1)]
    for block in range(1, RAW // SEG):
        pieces.append(raw[:, block * SEG - TILE : (block + 1) * SEG])
    spans = jnp.concatenate(pieces, 0)
    out = sum(contract(spans, part, 1, 1) for part in split3(band)[::-1])
    return jnp.concatenate([out[b * rows : (b + 1) * rows] for b in range(RAW // SEG)], 1)


def whiten_rows(decimated, keep, table_ref):
    high, low = split2(decimated)
    table_high = table_ref[:SEG, :]
    spectrum = contract(low, table_high, 1, 0) + contract(high, table_ref[SEG:, :], 1, 0)
    spectrum = spectrum + contract(high, table_high, 1, 0)
    real_part, imag_part = spectrum[:, :NBIN], spectrum[:, NBIN:]
    power = real_part * real_part + imag_part * imag_part
    level = jnp.mean(power, -1, keepdims=True)
    scale = keep.astype(jnp.float32) * lax.rsqrt(0.5 * power + 0.5 * level + 1e-05)
    return jnp.concatenate([real_part * scale, imag_part * scale], 1).astype(jnp.bfloat16)


def arrange(piece_ref, spectra_ref):
    members, rows = piece_ref.shape[:2]
    width = rows // WINDOWS
    for pair in range(WINDOWS // 2):
        for quarter in range(4):
            block = piece_ref[:, pair * 2 * width : (pair + 1) * 2 * width, quarter * 128 : (quarter + 1) * 128]
            block = block.astype(jnp.float32)
            for half in range(2):
                turned = block[:, half * width : (half + 1) * width].reshape(members * width, 128).T
                start = (quarter % 2) * 128 * 32 + (quarter // 2) * WINDOWS + pair * 2 + half
                spectra_ref[pl.ds(start, 128, 32), :] = turned


def stack_kernel(same, per_step, *refs):
    if same:
        rows_ref, lag_ref, out_ref, cross_ref, row_spec = refs
    else:
        _, rows_ref, cols_ref, lag_ref, out_ref, cross_ref, row_spec, col_spec = refs

    @pl.when(pl.program_id(0) == 0)
    def _():
        arrange(rows_ref, row_spec)
        if not same:
            arrange(cols_ref, col_spec)

        def one_bin(f, carry):
            start = pl.multiple_of(f * 32, 32)
            left = row_spec[pl.ds(start, 32), :]
            right = left if same else col_spec[pl.ds(start, 32), :]
            turned = jnp.concatenate([right[WINDOWS:], -right[:WINDOWS]], 0)
            both = jnp.concatenate([right, turned], 1).astype(jnp.bfloat16)
            cross = contract(left.astype(jnp.bfloat16), both, 0, 0)
            cross_ref[pl.ds(f, TILE, STRIDE), :] = cross[:, :TILE]
            cross_ref[pl.ds(f + NBIN, TILE, STRIDE), :] = cross[:, TILE:]
            return carry

        lax.fori_loop(0, NBIN, one_bin, 0, unroll=64)

    base = pl.program_id(0) * per_step
    for group in range(per_step // 4):
        picked = []
        for member in range(4):
            start = (base + group * 4 + member) * STRIDE
            picked.append(cross_ref[pl.ds(start, 2 * NBIN), :].astype(jnp.bfloat16))
        stacked = contract(jnp.concatenate(picked, 1), lag_ref[...], 0, 0)
        out_ref[group * 4 : group * 4 + 4] = stacked.reshape(4, TILE, LAGS).astype(jnp.bfloat16)


def stack(gathered, table):
    members = TILE * WINDOWS // gathered.shape[1]
    same = gathered.shape[0] == members
    per_step = 32
    block = (members,) + gathered.shape[1:]
    spectra = pltpu.VMEM((2 * NBIN * WINDOWS, TILE), jnp.float32)
    if same:
        prefetch = []
        sides = [pl.BlockSpec(block, lambda s: (0, 0, 0))]
    else:
        prefetch = [table[lax.axis_index("tiles")]]
        sides = [
            pl.BlockSpec(block, lambda s, entry: (entry[0], 0, 0)),
            pl.BlockSpec(block, lambda s, entry: (entry[1], 0, 0)),
        ]
    return pl.pallas_call(
        functools.partial(stack_kernel, same, per_step),
        out_shape=jax.ShapeDtypeStruct((TILE, TILE, LAGS), jnp.bfloat16),
        grid_spec=pltpu.PrefetchScalarGridSpec(
            num_scalar_prefetch=len(prefetch),
            grid=(TILE // per_step,),
            in_specs=sides + [pl.BlockSpec((2 * NBIN, LAGS), lambda s, *entry: (0, 0))],
            out_specs=pl.BlockSpec((per_step, TILE, LAGS), lambda s, *entry: (s, 0, 0)),
            scratch_shapes=[pltpu.VMEM((TILE * STRIDE, TILE), jnp.float32)] + [spectra] * len(sides),
        ),
        compiler_params=pltpu.CompilerParams(vmem_limit_bytes=60 << 20),
        cost_estimate=pl.CostEstimate(flops=10 << 30, bytes_accessed=12 << 20, transcendentals=0),
    )(*prefetch, *[gathered] * len(sides), lag_table())


def other_core(me):
    return me + 1 - 2 * (me % 2)


def other_chip(me):
    return me + 2 - 4 * ((me // 2) % 2)


def remote(source, target, send, receive, peer):
    return pltpu.make_async_remote_copy(
        src_ref=source,
        dst_ref=target,
        send_sem=send,
        recv_sem=receive,
        device_id={"tiles": peer},
        device_id_type=pl.DeviceIdType.MESH,
    )


def front_kernel(
    devices, raw_hbm, taps_ref, keep_ref, table_hbm, out_ref,
    raw_ref, table_ref, load_sem, sum_buf, part_buf, common_buf, held,
    part_send, part_recv, common_send, common_recv,
    right_send, left_send, chip_send, core_send, held_recv, local_sem,
):
    me = lax.axis_index("tiles")
    channels = raw_ref.shape[1]
    rows = WINDOWS * channels
    barrier = pltpu.get_barrier_semaphore()
    all_owners = devices == WINDOWS

    def greet(k, carry):
        pl.semaphore_signal(
            barrier, inc=1, device_id={"tiles": (me + k) % devices}, device_id_type=pl.DeviceIdType.MESH
        )
        return carry

    lax.fori_loop(1, devices, greet, 0)
    load_raw = pltpu.make_async_copy(raw_hbm, raw_ref, load_sem.at[0])
    load_raw.start()
    load_table = pltpu.make_async_copy(table_hbm, table_ref, load_sem.at[1])
    load_table.start()
    load_raw.wait()
    filtered = filter_rows(raw_ref, taps_ref).reshape(WINDOWS, channels, SEG)
    sum_buf[...] = jnp.sum(filtered, 1, keepdims=True)
    pl.semaphore_wait(barrier, devices - 1)

    def part_copy(owner, slot):
        return remote(sum_buf.at[owner], part_buf.at[slot], part_send.at[owner], part_recv.at[slot], owner)

    def common_copy(owner, peer):
        return remote(common_buf.at[owner], common_buf.at[owner], common_send.at[peer], common_recv.at[owner], peer)

    def send_part(k, carry):
        owner = (me + k) % WINDOWS

        @pl.when(owner != me)
        def _():
            part_copy(owner, me).start()

        return carry

    lax.fori_loop(1 if all_owners else 0, WINDOWS, send_part, 0)

    @pl.when(me < WINDOWS)
    def _():
        part_buf[me] = sum_buf[me]

        def take(k, carry):
            part_copy(me, (me + k) % devices).wait_recv()
            return carry

        lax.fori_loop(1, devices, take, 0)
        common_buf[me] = jnp.sum(part_buf[...], 0)

        def give(k, carry):
            common_copy(me, (me + k) % devices).start()
            return carry

        lax.fori_loop(1, devices, give, 0)

    def take_common(k, carry):
        owner = (me + k) % WINDOWS

        @pl.when(owner != me)
        def _():
            common_copy(owner, me).wait_recv()

        return carry

    lax.fori_loop(1 if all_owners else 0, WINDOWS, take_common, 0)
    common = common_buf[...] / (channels * devices)
    decimated = (filtered - common).reshape(rows, SEG)
    keep = jnp.broadcast_to(keep_ref[...].astype(jnp.float32).T[:, :, None], (WINDOWS, channels, NBIN))
    load_table.wait()
    whitened = whiten_rows(decimated, keep.reshape(rows, NBIN), table_ref)
    held[me] = whitened.reshape(PIECES, rows // PIECES, 2 * NBIN)

    depth = devices // 4
    q, low = me // 4, me % 4
    chip, core = other_chip(me), other_core(me)

    def block_copy(block, piece, send, peer):
        return remote(held.at[block, piece], held.at[block, piece], send, held_recv.at[block, piece], peer)

    def to_right(level, piece):
        return block_copy(4 * level + low, piece, right_send.at[level, piece], (me + 4) % devices)

    def to_left(level, piece):
        return block_copy(4 * level + low, piece, left_send.at[level, piece], (me + devices - 4) % devices)

    def to_chip(level, piece):
        return block_copy(4 * level + low, piece, chip_send.at[level, piece], chip)

    def to_core(block, piece):
        return block_copy(block, piece, core_send.at[block // 2, piece], core)

    def local_copy(block, piece):
        part = rows // PIECES
        return pltpu.make_async_copy(
            held.at[block, piece], out_ref.at[block, pl.ds(piece * part, part)], local_sem.at[block, piece]
        )

    def arrived(block, piece):
        to_core(block, piece).wait_recv()
        local_copy(block, piece).start()

    def line_block(level, piece, forward, go):
        block = 4 * level + low
        arrived(block, piece)

        @pl.when(go)
        def _():
            forward(level, piece).start()

        to_chip(level, piece).start()
        to_core(block, piece).start()

    def chip_block(level, piece):
        block = 4 * level + other_chip(low)
        arrived(block, piece)
        to_core(block, piece).start()

    for piece in range(PIECES):
        @pl.when(q < depth - 1)
        def _():
            to_right(q, piece).start()

        @pl.when(q > 0)
        def _():
            to_left(q, piece).start()

        to_chip(q, piece).start()

    for piece in range(PIECES):
        to_core(me, piece).start()
        local_copy(me, piece).start()

    def step(d, carry):
        for piece in range(PIECES):
            @pl.when(q - d >= 0)
            def _():
                line_block(q - d, piece, to_right, q < depth - 1)

            @pl.when(q + d < depth)
            def _():
                line_block(q + d, piece, to_left, q > 0)

        for piece in range(PIECES):
            @pl.when(d == 1)
            def _():
                chip_block(q, piece)

            @pl.when((d > 1) & (q - d + 1 >= 0))
            def _():
                chip_block(q - d + 1, piece)

            @pl.when((d > 1) & (q + d - 1 < depth))
            def _():
                chip_block(q + d - 1, piece)

        return carry

    lax.fori_loop(1, depth + 1, step, 0)

    def from_core(pair, carry):
        for piece in range(PIECES):
            arrived(2 * pair + core % 2, piece)
        return carry

    lax.fori_loop(0, 2 * depth, from_core, 0)

    def finish(level, carry):
        for piece in range(PIECES):
            @pl.when((level <= q) & (q < depth - 1))
            def _():
                to_right(level, piece).wait_send()

            @pl.when((level >= q) & (q > 0))
            def _():
                to_left(level, piece).wait_send()

            to_chip(level, piece).wait_send()
            to_core(4 * level + low, piece).wait_send()
            to_core(4 * level + other_chip(low), piece).wait_send()
        return carry

    lax.fori_loop(0, depth, finish, 0)

    def drain_part(k, carry):
        owner = (me + k) % WINDOWS

        @pl.when(owner != me)
        def _():
            part_copy(owner, me).wait_send()

        return carry

    lax.fori_loop(1 if all_owners else 0, WINDOWS, drain_part, 0)

    @pl.when(me < WINDOWS)
    def _():
        def drain(k, carry):
            common_copy(me, (me + k) % devices).wait_send()
            return carry

        lax.fori_loop(1, devices, drain, 0)

    def settle(block, carry):
        for piece in range(PIECES):
            local_copy(block, piece).wait()
        return carry

    lax.fori_loop(0, devices, settle, 0)


def front(devices, raw, fir, keep):
    rows = raw.shape[0] * raw.shape[1]
    depth = devices // 4
    dma = pltpu.SemaphoreType.DMA
    vmem = pl.BlockSpec(memory_space=pltpu.VMEM)
    hbm = pl.BlockSpec(memory_space=pl.ANY)
    line = pltpu.VMEM((WINDOWS, 1, SEG), jnp.float32)
    return pl.pallas_call(
        functools.partial(front_kernel, devices),
        out_shape=jax.ShapeDtypeStruct((devices, rows, 2 * NBIN), jnp.bfloat16),
        in_specs=[hbm, vmem, vmem, hbm],
        out_specs=pl.BlockSpec(memory_space=pl.ANY),
        scratch_shapes=[
            pltpu.VMEM(raw.shape, jnp.bfloat16), pltpu.VMEM((2 * SEG, 2 * NBIN), jnp.bfloat16), dma((2,)),
            line, pltpu.VMEM((devices, 1, SEG), jnp.float32), line,
            pltpu.VMEM((devices, PIECES, rows // PIECES, 2 * NBIN), jnp.bfloat16),
            dma((WINDOWS,)), dma((devices,)), dma((devices,)), dma((WINDOWS,)),
            dma((depth, PIECES)), dma((depth, PIECES)), dma((depth, PIECES)), dma((2 * depth, PIECES)),
            dma((devices, PIECES)), dma((devices, PIECES)),
        ],
        compiler_params=pltpu.CompilerParams(
            collective_id=0, has_side_effects=True, vmem_limit_bytes=60 << 20
        ),
    )(raw, fir.reshape(1, TAPS), keep.T, dft_tables())


def piece_tables():
    angle = 2.0 * np.pi / SEG * np.mod(np.arange(SEG)[:, None] * np.arange(NBIN)[None, :], SEG)
    bins = NBIN // PIECES
    cosine, sine = np.cos(angle).reshape(SEG, PIECES, bins), -np.sin(angle).reshape(SEG, PIECES, bins)
    table = np.concatenate([cosine, sine], 2).reshape(SEG, 2 * NBIN).astype(np.float32)
    high = table.astype(jnp.bfloat16)
    low = (table - high.astype(np.float32)).astype(jnp.bfloat16)
    return jnp.asarray(np.concatenate([high, low], 0))


def whiten_pieces(decimated, keep, table_ref):
    high, low = split2(decimated)
    table_high = table_ref[:SEG, :]
    spectrum = contract(low, table_high, 1, 0) + contract(high, table_ref[SEG:, :], 1, 0)
    spectrum = spectrum + contract(high, table_high, 1, 0)
    width = 2 * NBIN // PIECES
    parts = [spectrum[:, p * width : (p + 1) * width] for p in range(PIECES)]
    squares = [part * part for part in parts]
    level = jnp.sum(sum(squares), -1, keepdims=True) / NBIN
    whitened = []
    for part, square in zip(parts, squares):
        power = square + pltpu.roll(square, width // 2, 1)
        scale = keep * lax.rsqrt(0.5 * power + 0.5 * level + 1e-05)
        whitened.append((part * scale).astype(jnp.bfloat16))
    return whitened


PITCH = 33
HALF = TILE // 2
UPPER = HALF * STRIDE
NARROW = NBIN + 1
TURN = HALF + 1


def tile_kernel(
    devices, raw_hbm, taps_hbm, keep_hbm, table_hbm, cross_ref,
    raw_ref, taps_ref, keep_ref, table_ref, load_sem,
    sum_buf, pair_buf, chip_buf, common_buf, held, spectra_ref,
    pair_send, pair_recv, sum_send, sum_recv, common_send, common_recv,
    right_send, left_send, chip_send, core_send, held_recv,
):
    me = lax.axis_index("tiles")
    channels = raw_ref.shape[1]
    rows = WINDOWS * channels
    chips = devices // 2
    here, core = me // 2, me % 2
    partner = 2 * here + 1 - core
    barrier = pltpu.get_barrier_semaphore()

    def greet(device):
        pl.semaphore_signal(
            barrier, inc=1, device_id={"tiles": device}, device_id_type=pl.DeviceIdType.MESH
        )

    greet(partner)
    for k in range(1, chips):
        greet(2 * ((here + k) % chips) + core)
    load_raw = pltpu.make_async_copy(raw_hbm, raw_ref, load_sem.at[0])
    load_raw.start()
    load_taps = pltpu.make_async_copy(taps_hbm, taps_ref, load_sem.at[2])
    load_taps.start()
    load_keep = pltpu.make_async_copy(keep_hbm, keep_ref, load_sem.at[3])
    load_keep.start()
    load_table = pltpu.make_async_copy(table_hbm, table_ref, load_sem.at[1])
    load_table.start()
    load_taps.wait()
    load_raw.wait()
    filtered = filter_rows(raw_ref, taps_ref).reshape(WINDOWS, channels, SEG)
    sum_buf[...] = jnp.sum(filtered, 1).reshape(sum_buf.shape)
    pl.semaphore_wait(barrier, chips)

    pair = remote(sum_buf.at[1 - core], pair_buf, pair_send, pair_recv, partner)
    pair.start()
    pair.wait_recv()
    chip_buf[here] = sum_buf[core] + pair_buf[...]

    def sum_copy(chip, k):
        return remote(
            chip_buf.at[chip], chip_buf.at[chip], sum_send.at[k], sum_recv.at[chip], 2 * ((here + k) % chips) + core
        )

    for k in range(1, chips):
        sum_copy(here, k).start()
    for k in range(1, chips):
        sum_copy((here + k) % chips, k).wait_recv()
    common_buf[core] = jnp.sum(chip_buf[...], 0)

    def common_copy(half):
        return remote(common_buf.at[half], common_buf.at[half], common_send, common_recv, partner)

    common_copy(core).start()
    common_copy(1 - core).wait_recv()
    common = common_buf[...].reshape(WINDOWS, 1, SEG) / (channels * devices)
    decimated = (filtered - common).reshape(rows, SEG)
    load_keep.wait()
    keep = jnp.broadcast_to(keep_ref[...].astype(jnp.float32).T[:, :, None], (WINDOWS, channels, 128))
    load_table.wait()
    whitened = whiten_pieces(decimated, keep.reshape(rows, 128), table_ref)

    level, chip = me // 4, (me // 2) % 2
    last = devices // 4 - 1

    def at(line, chip_off, core_off):
        return 4 * line + 2 * (chip + chip_off - 2 * chip * chip_off) + core + core_off - 2 * core * core_off

    def block_copy(block, piece, send, peer):
        return remote(held.at[block, piece], held.at[block, piece], send, held_recv.at[block, piece], peer)

    def to_right(line, piece):
        return block_copy(at(line, 0, 0), piece, right_send.at[line, piece], (me + 4) % devices)

    def to_left(line, piece):
        return block_copy(at(line, 0, 0), piece, left_send.at[line, piece], (me + devices - 4) % devices)

    def to_chip(line, piece):
        return block_copy(at(line, 0, 0), piece, chip_send.at[line, piece], at(level, 1, 0))

    def to_core(line, chip_off, piece):
        return block_copy(at(line, chip_off, 0), piece, core_send.at[line, chip_off, piece], at(level, 0, 1))

    def arrived(line, chip_off, core_off, piece):
        block = at(line, chip_off, core_off)
        block_copy(block, piece, held_recv.at[block, piece], partner).wait_recv()

    def sides(d, action):
        pl.when(level >= d)(lambda: action(level - d, 1))
        pl.when(level + d <= last)(lambda: action(level + d, -1))

    def own(piece):
        pl.when(level < last)(lambda: to_right(level, piece).start())
        pl.when(level > 0)(lambda: to_left(level, piece).start())
        to_chip(level, piece).start()
        to_core(level, 0, piece).start()

    def line_step(d, piece):
        def take(line, sign):
            arrived(line, 0, 0, piece)
            if d < last:
                if sign > 0:
                    pl.when(level < last)(lambda: to_right(line, piece).start())
                else:
                    pl.when(level > 0)(lambda: to_left(line, piece).start())
            to_chip(line, piece).start()
            to_core(line, 0, piece).start()

        sides(d, take)

    def chip_step(d, piece):
        def take(line, sign):
            arrived(line, 1, 0, piece)
            to_core(line, 1, piece).start()

        if d == 0:
            take(level, 0)
        else:
            sides(d, take)

    def core_step(piece):
        for chip_off in range(2):
            for line in range(last + 1):
                arrived(line, chip_off, 1, piece)

    def drain_own():
        pair.wait_send()
        common_copy(core).wait_send()
        for k in range(1, chips):
            sum_copy(here, k).wait_send()
        for piece in range(PIECES):
            pl.when(level < last)(lambda: to_right(level, piece).wait_send())
            pl.when(level > 0)(lambda: to_left(level, piece).wait_send())
            to_chip(level, piece).wait_send()
            to_core(level, 0, piece).wait_send()
            to_core(level, 1, piece).wait_send()

    def drain_line(first, end):
        for d in range(first, end + 1):
            for piece in range(PIECES):
                def drain(line, sign):
                    if d < last:
                        if sign > 0:
                            pl.when(level < last)(lambda: to_right(line, piece).wait_send())
                        else:
                            pl.when(level > 0)(lambda: to_left(line, piece).wait_send())
                    to_chip(line, piece).wait_send()
                    to_core(line, 0, piece).wait_send()
                    to_core(line, 1, piece).wait_send()

                sides(d, drain)

    bins = NBIN // PIECES

    def turn(piece):
        for pair in range(WINDOWS // 2):
            block = held[:, piece, pair * 2 * channels : (pair + 1) * 2 * channels, :].astype(jnp.float32)
            for half in range(2):
                turned = block[:, half * channels : (half + 1) * channels].reshape(devices * channels, 2 * bins).T
                window = pair * 2 + half
                spectra_ref[piece % 2, pl.ds(window, bins, PITCH), :] = turned[:bins]
                spectra_ref[piece % 2, pl.ds(WINDOWS + window, bins, PITCH), :] = turned[bins:]

    def multiply(piece):
        span = 16 * WINDOWS
        place = lax.broadcasted_iota(jnp.int32, (HALF, span), 1) // (2 * WINDOWS)
        odd = lax.broadcasted_iota(jnp.int32, (span, TILE), 0) // (2 * WINDOWS) % 2
        upper = lax.broadcasted_iota(jnp.int32, (span, TILE), 1) < HALF

        def eight_bins(g):
            spans = [spectra_ref[piece % 2, pl.ds((g * 8 + k) * PITCH, 2 * WINDOWS), :] for k in range(8)]
            right = jnp.concatenate(spans, 0)
            split = right.reshape(8, 2, WINDOWS, TILE)
            turned = jnp.concatenate([split[:, 1:], -split[:, :1]], 1).reshape(span, TILE)
            both = jnp.concatenate([right, turned], 1).astype(jnp.bfloat16)
            narrow = jnp.where(upper, pltpu.roll(right, HALF, 1), turned)
            pairs = jnp.concatenate([jnp.where(odd == k, narrow, 0.0) for k in range(2)], 1).astype(jnp.bfloat16)
            left = right.T
            picked = [jnp.where(place == k, left[:HALF], 0.0).astype(jnp.bfloat16) for k in range(8)]
            wide = contract(jnp.concatenate(picked, 0), both, 1, 0)
            picked = [jnp.where(place // 2 == k, left[HALF:], 0.0).astype(jnp.bfloat16) for k in range(4)]
            paired = contract(jnp.concatenate(picked, 0), pairs, 1, 0)
            for k in range(8):
                f = piece * bins + g * 8 + k
                cross_ref[pl.ds(f, HALF, STRIDE), :] = wide[k * HALF : (k + 1) * HALF, :TILE]
                cross_ref[pl.ds(f + NBIN, HALF, STRIDE), :] = wide[k * HALF : (k + 1) * HALF, TILE:]
                column = k % 2 * TILE
                cross_ref[pl.ds(UPPER + f, HALF, NARROW), :] = paired[
                    k // 2 * HALF : (k // 2 + 1) * HALF, column : column + TILE
                ]

        for g in range(bins // 8):
            eight_bins(g)

    for piece in range(PIECES):
        held[me, piece] = whitened[piece]
        own(piece)
    for d in range(1, last + 1):
        if d == last:
            drain_own()
            drain_line(1, last - 2)
        for piece in range(PIECES):
            line_step(d, piece)
        for piece in range(PIECES):
            chip_step(d - 1, piece)
    chip_step(last, 0)
    chip_step(last, 1)
    core_step(0)
    turn(0)
    chip_step(last, 2)
    chip_step(last, 3)
    core_step(1)
    turn(1)
    multiply(0)
    core_step(2)
    core_step(3)
    turn(2)
    multiply(1)
    turn(3)
    multiply(2)
    multiply(3)

    drain_line(last - 1, last)


def tile_cross(devices, raw, fir, keep):
    rows = raw.shape[0] * raw.shape[1]
    dma = pltpu.SemaphoreType.DMA
    vmem = pl.BlockSpec(memory_space=pltpu.VMEM)
    hbm = pl.BlockSpec(memory_space=pltpu.HBM)
    half = (2, WINDOWS // 2, SEG)
    return pl.pallas_call(
        functools.partial(tile_kernel, devices),
        out_shape=pltpu.VMEM((UPPER + HALF * NARROW, TILE), jnp.float32),
        in_specs=[hbm] * 4,
        out_specs=vmem,
        scratch_shapes=[
            pltpu.VMEM(raw.shape, jnp.bfloat16), pltpu.VMEM((1, TAPS), jnp.float32),
            pltpu.VMEM(keep.shape[::-1], jnp.int32), pltpu.VMEM((2 * SEG, 2 * NBIN), jnp.bfloat16), dma((4,)),
            pltpu.VMEM(half, jnp.float32), pltpu.VMEM(half[1:], jnp.float32),
            pltpu.VMEM((devices // 2,) + half[1:], jnp.float32), pltpu.VMEM(half, jnp.float32),
            pltpu.VMEM((devices, PIECES, rows, 2 * NBIN // PIECES), jnp.bfloat16),
            pltpu.VMEM((2, PITCH * NBIN // PIECES, TILE), jnp.float32),
            dma, dma, dma((devices // 2,)), dma((devices // 2,)), dma, dma,
            dma((4, PIECES)), dma((4, PIECES)), dma((4, PIECES)), dma((4, 2, PIECES)), dma((devices, PIECES)),
        ],
        compiler_params=pltpu.CompilerParams(
            collective_id=0, has_side_effects=True, vmem_limit_bytes=10 << 20
        ),
    )(*[pltpu.with_memory_space_constraint(x, pltpu.HBM) for x in (raw, fir.reshape(1, TAPS), keep.T, piece_tables())])


def lag_kernel(per_step, cross_ref, lag_ref, out_ref, mirror_ref):
    base = pl.program_id(0) * per_step

    @pl.when(base < HALF)
    def _():
        for group in range(0, per_step, 4):
            turned = [
                cross_ref[pl.ds((base + group + k) * STRIDE, 2 * NBIN), :].astype(jnp.bfloat16).T for k in range(4)
            ]
            near = contract(jnp.concatenate([t[:HALF] for t in turned], 0), lag_ref[...], 1, 0)
            far = jnp.concatenate([t[HALF:] for t in turned], 0)
            even = contract(far[:, :NBIN], lag_ref[:NBIN, :], 1, 0)
            odd = contract(far[:, NBIN:], lag_ref[NBIN:, :], 1, 0)
            mirrored = even - odd
            out_ref[group : group + 4, :HALF] = near.reshape(4, HALF, LAGS).astype(jnp.bfloat16)
            out_ref[group : group + 4, HALF:] = (even + odd).reshape(4, HALF, LAGS).astype(jnp.bfloat16)
            for k in range(4):
                for part in range(LAGS // 128):
                    mirror_ref[part, pl.ds(base + group + k, HALF, TURN), :] = mirrored[
                        k * HALF : (k + 1) * HALF, part * 128 : (part + 1) * 128
                    ]

    @pl.when(base >= HALF)
    def _():
        for group in range(0, per_step, 4):
            rows = []
            for k in range(4):
                row = base - HALF + group + k
                turned = cross_ref[pl.ds(UPPER + row * NARROW, NBIN), :].astype(jnp.bfloat16).T
                rows.append(jnp.concatenate([turned[:HALF], turned[HALF:]], 1))
                parts = [mirror_ref[part, pl.ds(row * TURN, HALF), :] for part in range(LAGS // 128)]
                out_ref[group + k, :HALF] = jnp.concatenate(parts, 1).astype(jnp.bfloat16)
            far = contract(jnp.concatenate(rows, 0), lag_ref[...], 1, 0)
            out_ref[group : group + 4, HALF:] = far.reshape(4, HALF, LAGS).astype(jnp.bfloat16)


def tile_stack(cross):
    per_step = 64
    vmem = pl.BlockSpec(memory_space=pltpu.VMEM)
    return pl.pallas_call(
        functools.partial(lag_kernel, per_step),
        out_shape=jax.ShapeDtypeStruct((TILE, TILE, LAGS), jnp.bfloat16),
        grid=(TILE // per_step,),
        in_specs=[vmem, vmem],
        out_specs=pl.BlockSpec((per_step, TILE, LAGS), lambda s: (s, 0, 0)),
        scratch_shapes=[pltpu.VMEM((LAGS // 128, HALF * TURN, 128), jnp.float32)],
        compiler_params=pltpu.CompilerParams(vmem_limit_bytes=22 << 20),
        cost_estimate=pl.CostEstimate(flops=5 << 30, bytes_accessed=12 << 20, transcendentals=0),
    )(cross, lag_table())


def local(raw, fir, keep, table):
    devices = lax.axis_size("tiles")
    if devices == WINDOWS and devices * raw.shape[1] == TILE:
        return tile_stack(tile_cross(devices, raw, fir, keep))[None]
    gathered = front(devices, raw, fir, keep)
    return stack(gathered, table)[None]


def solution(mesh):
    placed = (P(None, ("groups", "tiles"), None), P(), P(None, ("groups", "tiles")), P())
    return jax.shard_map(
        local,
        mesh=mesh,
        in_specs=placed,
        out_specs=P(("groups", "tiles"), None, None, None),
        check_vma=False,
    )
```
